32 devices in a mesh: gx: 4 (over z), gy: 2 (over x), gz: 4 (over y, core).
Axes of the slice: x: 2, y: 2, z: 4, core: 2. Of those that a mesh axis runs over, the one named last changes fastest.
Arguments:
- element_state: float32 [9, 35, 4096], P(None, None, ('gx', 'gy', 'gz')), may hold values from -6 to 6
- jacobians: float32 [3, 9, 9, 4096], P(None, None, None, ('gx', 'gy', 'gz')), may hold values from -1.25 to 1.25
- stiffness: float32 [3, 35, 35], replicated, may hold values from -1 to 1
- projection: float32 [4, 15, 35], replicated, may hold values from -1 to 1
- flux_self: float32 [4, 9, 9, 4096], P(None, None, None, ('gx', 'gy', 'gz')), may hold values from -1 to 1
- flux_other: float32 [4, 9, 9, 4096], P(None, None, None, ('gx', 'gy', 'gz')), may hold values from -1 to 1
- face_source: int32 [4, 4096], P(None, ('gx', 'gy', 'gz')), may hold values from 0 to 607, as said below
- send_faces: int32 [6, 512], P(None, ('gx', 'gy', 'gz')), may hold values from 0 to 511
- cluster_mask: int32 [4096], P(('gx', 'gy', 'gz')), may hold values from 0 to 1
- seafloor_face: int32 [32768], P(('gx', 'gy', 'gz')), may hold values from -1 to 511, as said below
- ocean_cell: int32 [8, 4, 1024], P(('gx', 'gy')), may hold values from 0 to 65535
- ocean_weight: float32 [8, 4, 15, 1024], P(('gx', 'gy')), may hold values from 0 to 0.5
- height: float32 [1024, 512], P('gx', 'gy'), may hold values from -6 to 6
- east_flow: float32 [1024, 512], P('gx', 'gy'), may hold values from -6 to 6
- north_flow: float32 [1024, 512], P('gx', 'gy'), may hold values from -6 to 6
- water_depth: float32 [1024, 512], P('gx', 'gy'), may hold values from 0.5 to 2
Outputs:
- next_state: float32 [9, 35, 4096], P(None, None, ('gx', 'gy', 'gz'))
- new_height: float32 [1024, 512], P('gx', 'gy')
- new_east: float32 [1024, 512], P('gx', 'gy')
- new_north: float32 [1024, 512], P('gx', 'gy')
The draws below stay inside these ranges and needn't reach their ends.
Inputs may be any that keep to these rules, and one draw needn't show every extreme that they name: `face_source`: within a partition, each of the 96 received columns (numbered from 512) is named by exactly one face; all other faces name the partition's own trace columns. `seafloor_face`: values are local face numbers or -1 for an empty slot. In each block of 128 slots of one partition for one tile the live slots come first and at least one is live; for one tile, the block of every partition is full.
All inputs are finite; a program needn't handle non-finite values.
Results may differ from the reference program's by a relative error of at most 0.0003.
Values sent between devices are 32-bit elements; how exact they have to be, the bound alone decides.
A program may use at most 128 MiB of HBM per device.

```python
import math
import jax
import jax.numpy as jnp
from jax import lax

NQ = 9
NB = 35
NF = 15
E_DEV = 128
SLOTS = 128
CXO = 256
CYO = 256
BLOCK = 16
ELEMS = 4096
TILES = 8
NXO = 1024
NYO = 512
N_GX = 4
N_GY = 2
N_GZ = 4
DEVICES = 32


def draw_face_source(key, part):
    partitions = ELEMS // E_DEV
    device_keys = jax.random.split(key, partitions)

    def per_device(single_key):
        key_rank, key_local = jax.random.split(single_key)
        order_rank = jax.random.permutation(key_rank, 4 * E_DEV).astype(jnp.int32)
        local_face = jax.random.randint(key_local, (4 * E_DEV,), 0, 4 * E_DEV)
        chosen = jnp.where(order_rank < 6 * BLOCK, 4 * E_DEV + order_rank, local_face)
        return chosen.reshape(4, E_DEV)
    stacked = jax.vmap(per_device)(device_keys)
    return jnp.transpose(stacked, (1, 0, 2)).reshape(4, ELEMS).astype(jnp.int32)


def draw_seafloor_face(key, part):
    partitions = ELEMS // E_DEV
    key_full, key_count, key_face = jax.random.split(jax.random.fold_in(key, 17), 3)
    full_tile = jax.random.randint(key_full, (), 0, TILES)
    live_count = jax.random.randint(key_count, (partitions, TILES, 1), 1, SLOTS + 1)
    tile_ids = jnp.arange(TILES, dtype=jnp.int32)[None, :, None]
    live_count = jnp.where(tile_ids == full_tile, SLOTS, live_count)
    face_ids = jax.random.randint(key_face, (partitions, TILES, SLOTS), 0, 4 * E_DEV)
    slot_ids = jnp.arange(SLOTS, dtype=jnp.int32)[None, None, :]
    live = slot_ids < live_count
    return jnp.where(live, face_ids, -1).reshape(-1).astype(jnp.int32)


def draw_cluster_mask(key, part):
    partitions = ELEMS // E_DEV
    key_level, key_draw = jax.random.split(key)
    levels = jax.random.randint(key_level, (partitions, 1), 2, 9)
    rolled = jax.random.randint(key_draw, (partitions, E_DEV), 0, 8)
    return (rolled < levels).astype(jnp.int32).reshape(-1)


def touch_ends(entries, stream_key, low, top_value):
    longest = entries.shape.index(max(entries.shape))
    spots = []
    for shift in (0, 1):
        where = [jax.random.randint(jax.random.fold_in(stream_key, axis), (), 0, length) for axis, length in enumerate(entries.shape)]
        where[longest] = (where[longest] + shift) % entries.shape[longest]
        spots.append(tuple(where))
    return entries.at[spots[0]].set(low).at[spots[1]].set(top_value)


def block_levels(key, dims, pieces, smallest, top_value):
    level, own = 1.0, jax.random.fold_in(key, 6)
    for dim, blocks in pieces:
        steps = jnp.exp(jax.random.uniform(jax.random.fold_in(own, dim), (blocks,), jnp.float32, smallest / len(pieces), top_value / len(pieces)))
        level = level * jnp.repeat(steps, dims[dim] // blocks).reshape([-1 if axis == dim else 1 for axis in range(len(dims))])
    return level


def centred(key, extent, spread, limit, cuts=(), kind=jnp.bfloat16):
    entries = spread * jax.random.normal(key, extent, jnp.float32)
    if cuts:
        entries = entries * block_levels(key, extent, cuts, -0.22, 0.18)
    return jnp.clip(entries, -limit, limit).astype(kind)


def setup_inputs(seed: int = 0) -> dict:
    keys = jax.random.split(jax.random.key(seed), 17)
    return {
        "element_state": centred(keys[0], (NQ, NB, ELEMS), 1.0, 6.0, ((2, 32),), jnp.float32),
        "jacobians": centred(keys[1], (3, NQ, NQ, ELEMS), (3 * NQ) ** -0.5, 1.25, ((3, 32),), jnp.float32),
        "stiffness": centred(keys[2], (3, NB, NB), NB ** -0.5, 1.0, (), jnp.float32),
        "projection": centred(keys[3], (4, NF, NB), NB ** -0.5, 1.0, (), jnp.float32),
        "flux_self": centred(keys[4], (4, NQ, NQ, ELEMS), (4 * NQ) ** -0.5, 1.0, ((3, 32),), jnp.float32),
        "flux_other": centred(keys[5], (4, NQ, NQ, ELEMS), (4 * NQ) ** -0.5, 1.0, ((3, 32),), jnp.float32),
        "face_source": draw_face_source(jax.random.fold_in(keys[16], 71), 0),
        "send_faces": touch_ends(jax.random.randint(keys[7], (6, BLOCK * DEVICES), 0, 4 * E_DEV), jax.random.fold_in(keys[7], 1), 0, (4 * E_DEV) - 1).astype(jnp.int32),
        "cluster_mask": draw_cluster_mask(jax.random.fold_in(keys[16], 71), 0),
        "seafloor_face": draw_seafloor_face(jax.random.fold_in(keys[16], 71), 0),
        "ocean_cell": touch_ends(jax.random.randint(keys[10], (TILES, N_GZ, TILES * SLOTS), 0, CXO * CYO), jax.random.fold_in(keys[10], 1), 0, (CXO * CYO) - 1).astype(jnp.int32),
        "ocean_weight": jnp.clip(0.5 * jax.random.uniform(keys[11], (TILES, N_GZ, NF, TILES * SLOTS), jnp.float32) ** block_levels(keys[11], (TILES, N_GZ, NF, TILES * SLOTS), ((0, 8),), -0.2, 0.2), 0.0, 0.5),
        "height": centred(keys[12], (NXO, NYO), 1.0, 6.0, ((0, 4), (1, 2)), jnp.float32),
        "east_flow": centred(keys[13], (NXO, NYO), 1.0, 6.0, ((0, 4), (1, 2)), jnp.float32),
        "north_flow": centred(keys[14], (NXO, NYO), 1.0, 6.0, ((0, 4), (1, 2)), jnp.float32),
        "water_depth": jnp.clip(jnp.exp(math.log(2.0) - 1.3862944 * jax.random.uniform(keys[15], (NXO, NYO), jnp.float32) ** block_levels(keys[15], (NXO, NYO), ((0, 4), (1, 2)), -0.2, 0.2)), 0.5, 2.0),
    }


time_step = 1.5
ocean_step = 0.5
highest = lax.Precision.HIGHEST


def derivative(dof_state, jacobian_local, stiffness):
    coupled = jnp.einsum('dpqe,qbe->dpbe', jacobian_local, dof_state, precision=highest)
    return -jnp.einsum('dcb,dpbe->pce', stiffness, coupled, precision=highest)


def predictor(dof_state, jacobian_local, stiffness):
    weight_now = time_step
    integral = weight_now * dof_state
    current = dof_state
    for degree in range(1, 5):
        current = derivative(current, jacobian_local, stiffness)
        weight_now = weight_now * time_step / (degree + 1)
        integral = integral + weight_now * current
    return integral


def volume_term(integral, jacobian_local, stiffness):
    coupled = jnp.einsum('dpqe,qbe->dpbe', jacobian_local, integral, precision=highest)
    return jnp.einsum('dbc,dpbe->pce', stiffness, coupled, precision=highest)


def trace_table(integral, projection):
    traces = jnp.einsum('fab,qbe->qafe', projection, integral, precision=highest)
    return traces.reshape(NQ * NF, 4 * integral.shape[2])


def flux_term(trace_flat, neighbour_table, face_source, flux_self, flux_other, projection):
    element_count = face_source.shape[1]
    own_traces = trace_flat.reshape(NQ, NF, 4, element_count)
    result = jnp.zeros((NQ, NB, element_count), jnp.float32)
    for side_index in range(4):
        remote = jnp.take(neighbour_table, face_source[side_index], axis=1).reshape(NQ, NF, element_count)
        numeric = jnp.einsum('qae,qpe->pae', own_traces[:, :, side_index], flux_self[side_index], precision=highest)
        numeric = numeric + jnp.einsum('qae,qpe->pae', remote, flux_other[side_index], precision=highest)
        result = result + jnp.einsum('ab,pae->pbe', projection[side_index], numeric, precision=highest)
    return result


def uplift_trace(trace_flat, seafloor_face):
    is_live = seafloor_face >= 0
    face_index = jnp.maximum(seafloor_face, 0)
    vertical = trace_flat[8 * NF:9 * NF]
    picked = jnp.take(vertical, face_index, axis=1)
    return jnp.where(is_live[None, :], picked, 0.0)


def pressure_term(load_trace, seafloor_face, projection, element_count):
    is_live = seafloor_face >= 0
    face_index = jnp.maximum(seafloor_face, 0)
    side_of_face = face_index // element_count
    element_index = face_index % element_count
    weighted = jnp.where(is_live[None, :], load_trace, 0.0)
    lifted = jnp.zeros((NB, seafloor_face.shape[0]), jnp.float32)
    for side_index in range(4):
        chosen = jnp.where(side_of_face[None, :] == side_index, weighted, 0.0)
        lifted = lifted + jnp.dot(projection[side_index].T, chosen, precision=highest)
    return jnp.zeros((NB, element_count), jnp.float32).at[:, element_index].add(lifted)


def element_update(state_local, jacobian_local, stiffness, projection, self_local, other_local,
                   source_local, mask_local, floor_local, integral, trace_flat, received, load_trace):
    neighbour_table = jnp.concatenate([trace_flat, received], axis=1)
    volume = volume_term(integral, jacobian_local, stiffness)
    flux_sum = flux_term(trace_flat, neighbour_table, source_local, self_local, other_local, projection)
    pressure = pressure_term(load_trace, floor_local, projection, state_local.shape[2])
    updated = state_local + volume - flux_sum
    updated = updated.at[2].add(-pressure)
    return jnp.where(mask_local[None, None, :] > 0, updated, state_local)


def split_devices(whole_array, partitions):
    shaped = whole_array.reshape(whole_array.shape[:-1] + (partitions, whole_array.shape[-1] // partitions))
    return jnp.moveaxis(shaped, -2, 0)


def from_below(arranged, position):
    length = arranged.shape[position]
    kept_part = lax.slice_in_dim(arranged, 0, length - 1, axis=position)
    zeros_rim = jnp.zeros_like(lax.slice_in_dim(arranged, 0, 1, axis=position))
    return jnp.concatenate([zeros_rim, kept_part], axis=position)


def from_above(arranged, position):
    length = arranged.shape[position]
    kept_part = lax.slice_in_dim(arranged, 1, length, axis=position)
    zeros_rim = jnp.zeros_like(lax.slice_in_dim(arranged, 0, 1, axis=position))
    return jnp.concatenate([kept_part, zeros_rim], axis=position)


def ocean_update(height, east_flow, north_flow, water_depth, source):
    padded_east = jnp.pad(east_flow, 1)
    padded_north = jnp.pad(north_flow, 1)
    east_slope = (padded_east[2:, 1:-1] - padded_east[:-2, 1:-1]) * 0.5
    north_slope = (padded_north[1:-1, 2:] - padded_north[1:-1, :-2]) * 0.5
    height_next = height + ocean_step * (source - water_depth * (east_slope + north_slope))
    padded_height = jnp.pad(height_next, 1)
    east_next = east_flow - ocean_step * (padded_height[2:, 1:-1] - padded_height[:-2, 1:-1]) * 0.5
    north_next = north_flow - ocean_step * (padded_height[1:-1, 2:] - padded_height[1:-1, :-2]) * 0.5
    return height_next, east_next, north_next


def reference(element_state, jacobians, stiffness, projection, flux_self, flux_other, face_source,
              send_faces, cluster_mask, seafloor_face, ocean_cell, ocean_weight, height, east_flow,
              north_flow, water_depth):
    partitions = N_GX * N_GY * N_GZ
    state_dev = split_devices(element_state, partitions)
    jacobian_dev = split_devices(jacobians, partitions)
    send_dev = split_devices(send_faces, partitions)
    floor_dev = split_devices(seafloor_face, partitions)

    def first_section(inputs):
        state_local, jacobian_local, send_local, floor_local = inputs
        integral = predictor(state_local, jacobian_local, stiffness)
        trace_flat = trace_table(integral, projection)
        outgoing = jnp.stack([jnp.take(trace_flat, send_local[direction], axis=1) for direction in range(6)])
        return integral, outgoing, uplift_trace(trace_flat, floor_local)

    integral_dev, outgoing_dev, uplift_dev = lax.map(first_section, (state_dev, jacobian_dev, send_dev, floor_dev))

    arranged = outgoing_dev.reshape((N_GX, N_GY, N_GZ, 6) + outgoing_dev.shape[2:])
    received = jnp.stack([
        from_below(arranged[:, :, :, 1], 0), from_above(arranged[:, :, :, 0], 0),
        from_below(arranged[:, :, :, 3], 1), from_above(arranged[:, :, :, 2], 1),
        from_below(arranged[:, :, :, 5], 2), from_above(arranged[:, :, :, 4], 2)], axis=3)
    received = received.reshape((partitions, 6) + received.shape[4:])
    received = jnp.moveaxis(received, 1, 2).reshape(partitions, NQ * NF, -1)

    tile_count = N_GX * N_GY
    slots_all = tile_count * SLOTS

    def to_tiles(field_grid):
        return field_grid.reshape(N_GX, CXO, N_GY, CYO).transpose(0, 2, 1, 3).reshape(tile_count, CXO * CYO)

    def from_tiles(tiled_grid):
        return tiled_grid.reshape(N_GX, N_GY, CXO, CYO).transpose(0, 2, 1, 3).reshape(N_GX * CXO, N_GY * CYO)

    uplift_grid = uplift_dev.reshape(tile_count, N_GZ, NF, tile_count, SLOTS).transpose(3, 1, 2, 0, 4)
    uplift_grid = uplift_grid.reshape(tile_count, N_GZ, NF, slots_all)
    uplift_values = jnp.sum(ocean_weight * uplift_grid, axis=2).reshape(tile_count, N_GZ * slots_all)
    cells_flat = ocean_cell.reshape(tile_count, N_GZ * slots_all)

    def scatter_tile(cells_tile, values_tile):
        return jnp.zeros((CXO * CYO,), jnp.float32).at[cells_tile].add(values_tile)

    source = from_tiles(jax.vmap(scatter_tile)(cells_flat, uplift_values))

    def pick_tile(heights_tile, cells_tile):
        return jnp.take(heights_tile, cells_tile)

    heights_at = jax.vmap(pick_tile)(to_tiles(height), ocean_cell)
    load_grid = ocean_weight * heights_at[:, :, None, :]
    load_dev = load_grid.reshape(tile_count, N_GZ, NF, tile_count, SLOTS).transpose(3, 1, 2, 0, 4)
    load_dev = load_dev.reshape(partitions, NF, slots_all)

    def second_section(inputs):
        (state_local, jacobian_local, self_local, other_local, source_local, mask_local,
         floor_local, integral, received_local, load_local) = inputs
        trace_flat = trace_table(integral, projection)
        return element_update(state_local, jacobian_local, stiffness, projection, self_local, other_local,
                              source_local, mask_local, floor_local, integral, trace_flat,
                              received_local, load_local)

    next_dev = lax.map(second_section, (
        state_dev, jacobian_dev, split_devices(flux_self, partitions), split_devices(flux_other, partitions),
        split_devices(face_source, partitions), split_devices(cluster_mask, partitions), floor_dev,
        integral_dev, received, load_dev))
    next_state = jnp.moveaxis(next_dev, 0, -2).reshape(NQ, NB, -1)
    new_height, new_east, new_north = ocean_update(height, east_flow, north_flow, water_depth, source)
    return (next_state, new_height, new_east, new_north)
```

```python
import functools

import jax
import jax.numpy as jnp
from jax import lax
from jax.experimental import pallas as pl
from jax.experimental.pallas import tpu as pltpu
from jax.sharding import PartitionSpec as P

F32 = jnp.float32
BF16 = jnp.bfloat16
MESH = pl.DeviceIdType.MESH
time_step = 1.5
ocean_step = 0.5
NN = (((1,), (0,)), ((), ()))
NT = (((1,), (1,)), ((), ()))


def up(n, m):
    return -(-n // m) * m


def mm(a, b, dims=NN):
    return lax.dot_general(a, b, dims, preferred_element_type=F32)


def split(x):
    hi = x.astype(BF16)
    return hi, (x - hi.astype(F32)).astype(BF16)


def iota(shape, dim):
    return lax.broadcasted_iota(jnp.int32, shape, dim)


def ones_where(cond):
    return jnp.where(cond, 1.0, 0.0).astype(BF16)


def kernel(
    dims,
    state_ref,
    jac_ref,
    stiff_ref,
    proj_ref,
    self_ref,
    other_ref,
    source_ref,
    send_ref,
    mask_ref,
    floor_ref,
    cell_ref,
    weight_ref,
    height_ref,
    east_ref,
    north_ref,
    depth_ref,
    next_ref,
    new_height_ref,
    new_east_ref,
    new_north_ref,
    cur,
    integ,
    coup,
    lhs_d,
    lhs_v,
    lhs_p,
    lhs_t,
    table,
    numeric,
    floor_hot,
    face_hot,
    hot_c,
    w_out,
    w_in,
    v_out,
    v_in,
    faces_out,
    faces_in,
    flow_out,
    flow_in,
    rim_out,
    rim_in,
    w_send,
    w_recv,
    v_send,
    v_recv,
    f_send,
    f_recv,
    o_send,
    o_recv,
    r_send,
    r_recv,
):
    n_gx, n_gy, n_gz, nq, nb, nf, ne, slots, block = dims
    tiles = n_gx * n_gy
    devices = tiles * n_gz
    nbp, nfp = up(nb, 8), up(nf, 16)
    rows, cols = height_ref.shape
    i, j, k = lax.axis_index("gx"), lax.axis_index("gy"), lax.axis_index("gz")
    tile = i * n_gy + j
    me = tile * n_gz + k
    half = coup.shape[0]

    def place(n):
        return (n // (n_gy * n_gz), (n // n_gz) % n_gy, n % n_gz)

    barrier = pltpu.get_barrier_semaphore()

    @pl.loop(0, devices)
    def _(n):
        @pl.when(n != me)
        def _():
            pl.semaphore_signal(barrier, inc=1, device_id=place(n), device_id_type=MESH)

    tile_slots = tiles * slots
    group = min(tiles, 8)
    pieces = [slice(t * slots, (t + group) * slots) for t in range(0, tiles, group)]

    def in_row(layer, span):
        cells = cell_ref[0, pl.ds(layer, 1), span]
        return iota((rows, cells.shape[1]), 0) == cells // cols

    def in_col(layer, span):
        cells = cell_ref[0, pl.ds(layer, 1), span]
        return iota((cols, cells.shape[1]), 0) == cells % cols

    h_hi, h_lo = split(height_ref[...])
    for number, piece in enumerate(pieces):
        hot = ones_where(in_col(k, piece))
        picked = mm(h_hi, hot) + mm(h_lo, hot)
        heights = jnp.sum(jnp.where(in_row(k, piece), picked, 0.0), axis=0, keepdims=True)
        for part in range(group):
            t = number * group + part
            span = slice(t * slots, (t + 1) * slots)
            w_out[t, 0:nf, :] = weight_ref[0, k, :, span]
            w_out[t, nf : nf + 1, :] = heights[:, part * slots : (part + 1) * slots]

    square = iota((rows, cols), 0) == iota((rows, cols), 1)

    def as_row(column):
        return jnp.sum(jnp.where(square, column, 0.0), axis=0, keepdims=True)

    def as_column(row):
        return jnp.sum(jnp.where(square, row, 0.0), axis=1, keepdims=True)

    flow_out[0] = east_ref[0:1, :]
    flow_out[1] = east_ref[rows - 1 : rows, :]
    flow_out[2] = as_row(north_ref[:, 0:1])
    flow_out[3] = as_row(north_ref[:, cols - 1 : cols])

    pl.semaphore_wait(barrier, devices - 1)

    there = (i > 0, i < n_gx - 1, j > 0, j < n_gy - 1, k > 0, k < n_gz - 1)
    who = ((i - 1, j, k), (i + 1, j, k), (i, j - 1, k), (i, j + 1, k), (i, j, k - 1), (i, j, k + 1))

    def exchange(out, into, send, recv, direction):
        return pltpu.make_async_remote_copy(
            src_ref=out.at[direction],
            dst_ref=into.at[direction ^ 1],
            send_sem=send.at[direction],
            recv_sem=recv.at[direction ^ 1],
            device_id=who[direction],
            device_id_type=MESH,
        )

    def start_exchange(out, into, send, recv, count):
        for direction in range(count):

            @pl.when(there[direction])
            def _():
                exchange(out, into, send, recv, direction).start()

            @pl.when(jnp.logical_not(there[direction]))
            def _():
                into[direction] = jnp.zeros(into.shape[1:], F32)

    def end_exchange(out, into, send, recv, count):
        for direction in range(count):

            @pl.when(there[direction])
            def _():
                exchange(out, into, send, recv, direction).wait_send()
                pltpu.make_async_remote_copy(
                    src_ref=out.at[direction],
                    dst_ref=into.at[direction],
                    send_sem=send.at[direction],
                    recv_sem=recv.at[direction],
                    device_id=who[direction],
                    device_id_type=MESH,
                ).wait_recv()

    def weights_to(t, slot):
        return pltpu.make_async_remote_copy(
            src_ref=w_out.at[t],
            dst_ref=w_in.at[slot],
            send_sem=w_send.at[t],
            recv_sem=w_recv.at[slot],
            device_id=(t // n_gy, t % n_gy, k),
            device_id_type=MESH,
        )

    @pl.loop(0, tiles)
    def _(t):
        @pl.when(t != tile)
        def _():
            weights_to(t, tile).start()

    start_exchange(flow_out, flow_in, o_send, o_recv, 4)
    w_in[tile] = w_out[tile]

    for ref in (lhs_d, lhs_v, lhs_p, lhs_t, coup, cur, integ):
        ref[...] = jnp.zeros(ref.shape, ref.dtype)
    eye_b = ones_where(iota((nbp, nb), 0) == iota((nbp, nb), 1))

    def spots(count, width, first, second):
        r, c = iota((count, width), 0), iota((count, width), 1)
        once = c == first + r
        return ones_where(once | (c == second + r)), ones_where(once)

    total_d = jnp.zeros((nbp, 2 * half), F32)
    total_dl, total_v, total_vl = total_d, total_d, total_d
    for d in range(3):
        both, once = spots(nb, 2 * half, d * nbp, half + d * nbp)
        s_hi, s_lo = split(stiff_ref[d])
        total_d += mm(mm(eye_b, s_hi).astype(BF16), both)
        total_dl += mm(mm(eye_b, s_lo).astype(BF16), once)
        total_v += mm(mm(eye_b, s_hi, NT).astype(BF16), both)
        total_vl += mm(mm(eye_b, s_lo, NT).astype(BF16), once)
    lhs_d[0:nbp, :] = -total_d
    lhs_d[nbp : 2 * nbp, :] = -total_dl
    lhs_v[0:nbp, :] = total_v
    lhs_v[nbp : 2 * nbp, :] = total_vl

    nbk = integ.shape[0]
    faces = 4 * nfp
    both_b, once_b = spots(nb, 2 * nbk, 0, nbk)
    total_t = jnp.zeros((nbp, 2 * faces), F32)
    total_tl = total_t
    for f in range(4):
        both, once = spots(nf, 2 * faces, f * nfp, faces + f * nfp)
        p_hi, p_lo = split(proj_ref[f])
        lhs_p[f * nfp : f * nfp + nf, :] = mm(p_hi, both_b)
        lhs_p[faces + f * nfp : faces + f * nfp + nf, :] = mm(p_lo, once_b)
        total_t += mm(mm(eye_b, p_hi, NT).astype(BF16), both)
        total_tl += mm(mm(eye_b, p_lo, NT).astype(BF16), once)
    lhs_t[0:nbp, :] = total_t
    lhs_t[nbp : 2 * nbp, :] = total_tl

    def halves(lhs, rhs):
        hi, lo = split(rhs)
        out = mm(lhs[...].astype(BF16), jnp.concatenate([hi, lo], axis=0))
        count = out.shape[0] // 2
        return out[:count] + out[count:]

    for q in range(nq):
        cur[0:nb, q * ne : (q + 1) * ne] = state_ref[q]
    integ[0:nbp, :] = time_step * cur[...]

    def couple(values):
        @pl.loop(0, nq)
        def _(p):
            lane = pl.ds(pl.multiple_of(p * ne, ne), ne)
            sums = [None] * 3
            for q in range(nq):
                value = values[0:nbp, q * ne : (q + 1) * ne]
                for d in range(3):
                    term = jac_ref[d, p, q : q + 1, :] * value
                    sums[d] = term if q == 0 else sums[d] + term
            for d in range(3):
                coup[d * nbp : (d + 1) * nbp, lane] = sums[d]

    weight_now = time_step
    for degree in range(1, 5):
        couple(cur)
        weight_now = weight_now * time_step / (degree + 1)
        moved = halves(lhs_d, coup[...])
        if degree < 4:
            cur[...] = moved
        integ[0:nbp, :] += weight_now * moved

    traces = halves(lhs_p, integ[...])
    for q in range(nq):
        for f in range(4):
            table[q * nfp : (q + 1) * nfp, f * ne : (f + 1) * ne] = traces[
                f * nfp : (f + 1) * nfp, q * ne : (q + 1) * ne
            ]
    t_hi, t_lo = split(table[...])

    sends = 6 * block
    pick = ones_where(iota((sends, 6), 0) // block == iota((sends, 6), 1))
    index = send_ref[...]
    high = mm(pick, (index // 16).astype(F32).astype(BF16))
    low = mm(pick, (index % 16).astype(F32).astype(BF16))
    which = iota((sends, block), 0) % block == iota((sends, block), 1)
    chosen = jnp.sum(jnp.where(which, high * 16.0 + low, 0.0), axis=1, keepdims=True)
    send_hot = ones_where(iota((sends, 4 * ne), 1) == chosen.astype(jnp.int32))
    outgoing = mm(send_hot, t_hi, NT) + mm(send_hot, t_lo, NT)
    for direction in range(6):
        faces_out[direction] = outgoing[direction * block : (direction + 1) * block, :]
    start_exchange(faces_out, faces_in, f_send, f_recv, 6)

    for piece in pieces:
        floors = floor_ref[:, piece]
        floor_hot[:, piece] = ones_where(iota((4 * ne, floors.shape[1]), 0) == floors)
    vertical = slice((nq - 1) * nfp, nq * nfp)
    uptrace = mm(t_hi[vertical], floor_hot[...]) + mm(t_lo[vertical], floor_hot[...])

    @pl.loop(0, tiles)
    def _(t):
        @pl.when(t != tile)
        def _():
            weights_to(t, t).wait()

    for t in range(tiles):
        v_out[t] = jnp.sum(
            w_in[t, 0:nf, :] * uptrace[0:nf, t * slots : (t + 1) * slots], axis=0, keepdims=True
        )

    def values_to(n, slot):
        return pltpu.make_async_remote_copy(
            src_ref=v_out.at[n // n_gz],
            dst_ref=v_in.at[slot],
            send_sem=v_send.at[n],
            recv_sem=v_recv.at[slot],
            device_id=place(n),
            device_id_type=MESH,
        )

    mine = k * tiles + tile

    @pl.loop(0, devices)
    def _(n):
        @pl.when(n != me)
        def _():
            values_to(n, mine).start()

    v_in[mine] = v_out[tile]

    @pl.loop(0, n_gz)
    def _(layer):
        for span in pieces:
            hot_c[layer, :, span] = ones_where(in_col(layer, span))

    couple(integ)
    volume = halves(lhs_v, coup[...])

    @pl.loop(0, nq)
    def _(p):
        lane = pl.ds(pl.multiple_of(p * ne, ne), ne)
        for f in range(4):
            total = None
            for q in range(nq):
                own = table[q * nfp : (q + 1) * nfp, f * ne : (f + 1) * ne]
                term = self_ref[f, q, pl.ds(p, 1), :] * own
                total = term if q == 0 else total + term
            numeric[f * nfp : (f + 1) * nfp, lane] = total

    loads = jnp.concatenate(
        [w_in[t] * w_in[t, nf : nf + 1, :] for t in range(tiles)], axis=1
    )
    l_hi, l_lo = split(loads)
    face_load = mm(l_hi, floor_hot[...], NT) + mm(l_lo, floor_hot[...], NT)
    for f in range(4):
        numeric[f * nfp : f * nfp + nf, 2 * ne : 3 * ne] += face_load[
            0:nf, f * ne : (f + 1) * ne
        ]

    for f in range(4):
        face_hot[:, f * ne : (f + 1) * ne] = ones_where(
            iota((face_hot.shape[0], ne), 0) == source_ref[f : f + 1, :]
        )
    hot_own = face_hot[0 : 4 * ne, :]
    remote = mm(t_hi, hot_own) + mm(t_lo, hot_own)
    end_exchange(faces_out, faces_in, f_send, f_recv, 6)
    arrived = jnp.concatenate([faces_in[direction] for direction in range(6)], axis=0)
    a_hi, a_lo = split(arrived)
    width = nq * nfp
    eye_t = ones_where(iota((width, width), 0) == iota((width, width), 1))
    hot_far = face_hot[4 * ne : 4 * ne + sends, :]
    remote = remote + mm(mm(eye_t, a_hi, NT).astype(BF16), hot_far)
    remote = remote + mm(mm(eye_t, a_lo, NT).astype(BF16), hot_far)
    table[...] = remote

    @pl.loop(0, nq)
    def _(p):
        lane = pl.ds(pl.multiple_of(p * ne, ne), ne)
        for f in range(4):
            total = numeric[f * nfp : (f + 1) * nfp, lane]
            for q in range(nq):
                far = table[q * nfp : (q + 1) * nfp, f * ne : (f + 1) * ne]
                total = total + other_ref[f, q, pl.ds(p, 1), :] * far
            numeric[f * nfp : (f + 1) * nfp, lane] = total

    change = volume - halves(lhs_t, numeric[...])
    finest = mask_ref[...] > 0
    for q in range(nq):
        state = state_ref[q]
        next_ref[q] = jnp.where(finest, state + change[0:nb, q * ne : (q + 1) * ne], state)

    end_exchange(flow_out, flow_in, o_send, o_recv, 4)
    first_row, last_row = iota((rows, cols), 0) == 0, iota((rows, cols), 0) == rows - 1
    first_col, last_col = iota((rows, cols), 1) == 0, iota((rows, cols), 1) == cols - 1

    def slope_x(grid, rim):
        before = jnp.where(first_row, rim[0], pltpu.roll(grid, 1, 0))
        after = jnp.where(last_row, rim[1], pltpu.roll(grid, rows - 1, 0))
        return (after - before) * 0.5

    def slope_y(grid, rim):
        before = jnp.where(first_col, as_column(rim[2]), pltpu.roll(grid, 1, 1))
        after = jnp.where(last_col, as_column(rim[3]), pltpu.roll(grid, cols - 1, 1))
        return (after - before) * 0.5

    slopes = slope_x(east_ref[...], flow_in) + slope_y(north_ref[...], flow_in)
    base = height_ref[...] - ocean_step * (depth_ref[...] * slopes)

    @pl.loop(0, devices)
    def _(n):
        @pl.when(n != me)
        def _():
            values_to(n, (n % n_gz) * tiles + n // n_gz).wait()

    source = jnp.zeros((rows, cols), F32)
    for layer in range(n_gz):
        for number, piece in enumerate(pieces):
            first = layer * tiles + number * group
            values = jnp.concatenate([v_in[first + part] for part in range(group)], axis=1)
            v_hi, v_lo = split(values)
            here, other = in_row(layer, piece), hot_c[layer, :, piece]
            for part in (v_hi, v_lo):
                spread = jnp.where(here, part.astype(F32), 0.0).astype(BF16)
                source += mm(spread, other, NT)
    new_height = base + ocean_step * source
    rim_out[0] = new_height[0:1, :]
    rim_out[1] = new_height[rows - 1 : rows, :]
    rim_out[2] = as_row(new_height[:, 0:1])
    rim_out[3] = as_row(new_height[:, cols - 1 : cols])
    start_exchange(rim_out, rim_in, r_send, r_recv, 4)
    new_height_ref[...] = new_height
    end_exchange(rim_out, rim_in, r_send, r_recv, 4)
    new_east_ref[...] = east_ref[...] - ocean_step * slope_x(new_height, rim_in)
    new_north_ref[...] = north_ref[...] - ocean_step * slope_y(new_height, rim_in)


def on_device(
    sizes,
    element_state,
    jacobians,
    stiffness,
    projection,
    flux_self,
    flux_other,
    face_source,
    send_faces,
    cluster_mask,
    seafloor_face,
    ocean_cell,
    ocean_weight,
    height,
    east_flow,
    north_flow,
    water_depth,
):
    n_gx, n_gy, n_gz = sizes
    nq, nb, ne = element_state.shape
    nf = projection.shape[1]
    tiles = n_gx * n_gy
    devices = tiles * n_gz
    slots = seafloor_face.shape[0] // tiles
    block = send_faces.shape[1]
    rows, cols = height.shape
    nbp, nfp = up(nb, 8), up(nf, 16)
    half = up(3 * nbp, 16)
    nbk = up(nb, 16)
    faces = 4 * nfp
    args = (
        element_state,
        jacobians,
        stiffness,
        projection,
        flux_self,
        flux_other,
        face_source,
        send_faces,
        cluster_mask.reshape(1, -1),
        seafloor_face.reshape(1, -1),
        ocean_cell,
        ocean_weight,
        height,
        east_flow,
        north_flow,
        water_depth,
    )
    scratch = [
        pltpu.VMEM((nbp, nq * ne), F32),
        pltpu.VMEM((nbk, nq * ne), F32),
        pltpu.VMEM((half, nq * ne), F32),
        pltpu.VMEM((2 * nbp, 2 * half), F32),
        pltpu.VMEM((2 * nbp, 2 * half), F32),
        pltpu.VMEM((2 * faces, 2 * nbk), F32),
        pltpu.VMEM((2 * nbp, 2 * faces), F32),
        pltpu.VMEM((nq * nfp, 4 * ne), F32),
        pltpu.VMEM((faces, nq * ne), F32),
        pltpu.VMEM((4 * ne, tiles * slots), BF16),
        pltpu.VMEM((up(4 * ne + 6 * block, 16), 4 * ne), BF16),
        pltpu.VMEM((n_gz, cols, tiles * slots), BF16),
        pltpu.VMEM((tiles, nfp, slots), F32),
        pltpu.VMEM((tiles, nfp, slots), F32),
        pltpu.VMEM((tiles, 1, slots), F32),
        pltpu.VMEM((devices, 1, slots), F32),
        pltpu.VMEM((6, block, nq * nfp), F32),
        pltpu.VMEM((6, block, nq * nfp), F32),
        pltpu.VMEM((4, 1, cols), F32),
        pltpu.VMEM((4, 1, cols), F32),
        pltpu.VMEM((4, 1, cols), F32),
        pltpu.VMEM((4, 1, cols), F32),
    ]
    for count in (tiles, devices, 6, 4, 4):
        scratch += [pltpu.SemaphoreType.DMA((count,)), pltpu.SemaphoreType.DMA((count,))]
    return pl.pallas_call(
        functools.partial(kernel, (n_gx, n_gy, n_gz, nq, nb, nf, ne, slots, block)),
        out_shape=(
            jax.ShapeDtypeStruct(element_state.shape, F32),
            jax.ShapeDtypeStruct(height.shape, F32),
            jax.ShapeDtypeStruct(height.shape, F32),
            jax.ShapeDtypeStruct(height.shape, F32),
        ),
        in_specs=[pl.BlockSpec(memory_space=pltpu.VMEM)] * len(args),
        out_specs=[pl.BlockSpec(memory_space=pltpu.VMEM)] * 4,
        scratch_shapes=scratch,
        compiler_params=pltpu.CompilerParams(collective_id=0, has_side_effects=True),
        name="step",
    )(*args)


def solution(mesh):
    sizes = tuple(mesh.shape[axis] for axis in ("gx", "gy", "gz"))
    return jax.shard_map(
        functools.partial(on_device, sizes),
        mesh=mesh,
        in_specs=(
            P(None, None, ("gx", "gy", "gz")),
            P(None, None, None, ("gx", "gy", "gz")),
            P(),
            P(),
            P(None, None, None, ("gx", "gy", "gz")),
            P(None, None, None, ("gx", "gy", "gz")),
            P(None, ("gx", "gy", "gz")),
            P(None, ("gx", "gy", "gz")),
            P(("gx", "gy", "gz")),
            P(("gx", "gy", "gz")),
            P(("gx", "gy"), None, None),
            P(("gx", "gy"), None, None, None),
            P("gx", "gy"),
            P("gx", "gy"),
            P("gx", "gy"),
            P("gx", "gy"),
        ),
        out_specs=(P(None, None, ("gx", "gy", "gz")), P("gx", "gy"), P("gx", "gy"), P("gx", "gy")),
        check_vma=False,
    )
```

```python
import functools

import jax
import jax.numpy as jnp
from jax import lax
from jax.experimental import pallas as pl
from jax.experimental.pallas import tpu as pltpu
from jax.sharding import PartitionSpec as P

F32 = jnp.float32
BF16 = jnp.bfloat16
MESH = pl.DeviceIdType.MESH
time_step = 1.5
ocean_step = 0.5
NN = (((1,), (0,)), ((), ()))
NT = (((1,), (1,)), ((), ()))


def up(n, m):
    return -(-n // m) * m


def mm(a, b, dims=NN):
    return lax.dot_general(a, b, dims, preferred_element_type=F32)


def split(x):
    hi = x.astype(BF16)
    return hi, (x - hi.astype(F32)).astype(BF16)


def iota(shape, dim):
    return lax.broadcasted_iota(jnp.int32, shape, dim)


def ones_where(cond):
    return jnp.where(cond, 1.0, 0.0).astype(BF16)


def slopers(rows, cols):
    square = iota((rows, cols), 0) == iota((rows, cols), 1)

    def as_column(row):
        return jnp.sum(jnp.where(square, row, 0.0), axis=1, keepdims=True)

    first_row, last_row = iota((rows, cols), 0) == 0, iota((rows, cols), 0) == rows - 1
    first_col, last_col = iota((rows, cols), 1) == 0, iota((rows, cols), 1) == cols - 1

    def slope_x(grid, rim):
        before = jnp.where(first_row, rim[0], pltpu.roll(grid, 1, 0))
        after = jnp.where(last_row, rim[1], pltpu.roll(grid, rows - 1, 0))
        return (after - before) * 0.5

    def slope_y(grid, rim):
        before = jnp.where(first_col, as_column(rim[2]), pltpu.roll(grid, 1, 1))
        after = jnp.where(last_col, as_column(rim[3]), pltpu.roll(grid, cols - 1, 1))
        return (after - before) * 0.5

    return slope_x, slope_y


def kernel(
    dims,
    state_ref,
    jac_ref,
    stiff_ref,
    proj_ref,
    self_hbm,
    other_hbm,
    source_ref,
    send_ref,
    floor_ref,
    cell_ref,
    weight_ref,
    height_hbm,
    east_hbm,
    north_hbm,
    depth_hbm,
    change_ref,
    new_height_ref,
    rim_ref,
    cur,
    integ,
    coup,
    lhs_d,
    lhs_v,
    lhs_p,
    lhs_t,
    table,
    numeric,
    floor_hot,
    face_hot,
    hot_c,
    w_out,
    w_in,
    v_out,
    v_in,
    faces_out,
    faces_in,
    flow_out,
    flow_in,
    rim_out,
    rim_in,
    w_send,
    w_recv,
    v_send,
    v_recv,
    f_send,
    f_recv,
    o_send,
    o_recv,
    r_send,
    r_recv,
    self_ref,
    other_ref,
    height_ref,
    east_ref,
    north_ref,
    depth_ref,
    in_sem,
):
    n_gx, n_gy, n_gz, nq, nb, nf, ne, slots, block = dims
    tiles = n_gx * n_gy
    devices = tiles * n_gz
    nbp, nfp = up(nb, 8), up(nf, 16)
    rows, cols = height_ref.shape
    i, j, k = lax.axis_index("gx"), lax.axis_index("gy"), lax.axis_index("gz")
    tile = i * n_gy + j
    me = tile * n_gz + k
    half = coup.shape[0]

    def place(n):
        return (n // (n_gy * n_gz), (n // n_gz) % n_gy, n % n_gz)

    barrier = pltpu.get_barrier_semaphore()

    @pl.loop(0, devices)
    def _(n):
        @pl.when(n != me)
        def _():
            pl.semaphore_signal(barrier, inc=1, device_id=place(n), device_id_type=MESH)

    loads_in = [
        pltpu.make_async_copy(source, target, in_sem.at[number])
        for number, (source, target) in enumerate(
            (
                (height_hbm, height_ref),
                (east_hbm, east_ref),
                (north_hbm, north_ref),
                (self_hbm, self_ref),
                (depth_hbm, depth_ref),
                (other_hbm, other_ref),
            )
        )
    ]
    for load in loads_in:
        load.start()

    tile_slots = tiles * slots
    group = min(tiles, 8)
    pieces = [slice(t * slots, (t + group) * slots) for t in range(0, tiles, group)]

    def in_row(layer, span):
        cells = cell_ref[0, pl.ds(layer, 1), span]
        return iota((rows, cells.shape[1]), 0) == cells // cols

    def in_col(layer, span):
        cells = cell_ref[0, pl.ds(layer, 1), span]
        return iota((cols, cells.shape[1]), 0) == cells % cols

    square = iota((rows, cols), 0) == iota((rows, cols), 1)

    def as_row(column):
        return jnp.sum(jnp.where(square, column, 0.0), axis=0, keepdims=True)

    there = (i > 0, i < n_gx - 1, j > 0, j < n_gy - 1, k > 0, k < n_gz - 1)
    who = ((i - 1, j, k), (i + 1, j, k), (i, j - 1, k), (i, j + 1, k), (i, j, k - 1), (i, j, k + 1))

    def exchange(out, into, send, recv, direction):
        return pltpu.make_async_remote_copy(
            src_ref=out.at[direction],
            dst_ref=into.at[direction ^ 1],
            send_sem=send.at[direction],
            recv_sem=recv.at[direction ^ 1],
            device_id=who[direction],
            device_id_type=MESH,
        )

    def start_exchange(out, into, send, recv, count):
        for direction in range(count):

            @pl.when(there[direction])
            def _():
                exchange(out, into, send, recv, direction).start()

            @pl.when(jnp.logical_not(there[direction]))
            def _():
                into[direction] = jnp.zeros(into.shape[1:], F32)

    def end_exchange(out, into, send, recv, count):
        for direction in range(count):

            @pl.when(there[direction])
            def _():
                exchange(out, into, send, recv, direction).wait_send()
                pltpu.make_async_remote_copy(
                    src_ref=out.at[direction],
                    dst_ref=into.at[direction],
                    send_sem=send.at[direction],
                    recv_sem=recv.at[direction],
                    device_id=who[direction],
                    device_id_type=MESH,
                ).wait_recv()

    def weights_to(t, slot):
        return pltpu.make_async_remote_copy(
            src_ref=w_out.at[t],
            dst_ref=w_in.at[slot],
            send_sem=w_send.at[t],
            recv_sem=w_recv.at[slot],
            device_id=(t // n_gy, t % n_gy, k),
            device_id_type=MESH,
        )

    for ref in (lhs_d, lhs_v, lhs_p, lhs_t, coup, cur, integ):
        ref[...] = jnp.zeros(ref.shape, ref.dtype)
    eye_b = ones_where(iota((nbp, nb), 0) == iota((nbp, nb), 1))

    def spots(count, width, first, second):
        r, c = iota((count, width), 0), iota((count, width), 1)
        once = c == first + r
        return ones_where(once | (c == second + r)), ones_where(once)

    total_d = jnp.zeros((nbp, 2 * half), F32)
    total_dl, total_v, total_vl = total_d, total_d, total_d
    for d in range(3):
        both, once = spots(nb, 2 * half, d * nbp, half + d * nbp)
        s_hi, s_lo = split(stiff_ref[d])
        total_d += mm(mm(eye_b, s_hi).astype(BF16), both)
        total_dl += mm(mm(eye_b, s_lo).astype(BF16), once)
        total_v += mm(mm(eye_b, s_hi, NT).astype(BF16), both)
        total_vl += mm(mm(eye_b, s_lo, NT).astype(BF16), once)
    lhs_d[0:nbp, :] = -total_d
    lhs_d[nbp : 2 * nbp, :] = -total_dl
    lhs_v[0:nbp, :] = total_v
    lhs_v[nbp : 2 * nbp, :] = total_vl

    nbk = integ.shape[0]
    faces = 4 * nfp
    both_b, once_b = spots(nb, 2 * nbk, 0, nbk)
    total_t = jnp.zeros((nbp, 2 * faces), F32)
    total_tl = total_t
    for f in range(4):
        both, once = spots(nf, 2 * faces, f * nfp, faces + f * nfp)
        p_hi, p_lo = split(proj_ref[:, f, :])
        lhs_p[f * nfp : f * nfp + nf, :] = mm(p_hi, both_b)
        lhs_p[faces + f * nfp : faces + f * nfp + nf, :] = mm(p_lo, once_b)
        total_t += mm(mm(eye_b, p_hi, NT).astype(BF16), both)
        total_tl += mm(mm(eye_b, p_lo, NT).astype(BF16), once)
    lhs_t[0:nbp, :] = total_t
    lhs_t[nbp : 2 * nbp, :] = total_tl

    def halves(lhs, rhs):
        hi, lo = split(rhs)
        out = mm(lhs[...].astype(BF16), jnp.concatenate([hi, lo], axis=0))
        count = out.shape[0] // 2
        return out[:count] + out[count:]

    for q in range(nq):
        cur[0:nb, q * ne : (q + 1) * ne] = state_ref[q]
    integ[0:nbp, :] = time_step * cur[...]

    def couple(values):
        @pl.loop(0, nq)
        def _(p):
            lane = pl.ds(pl.multiple_of(p * ne, ne), ne)
            sums = [None] * 3
            for q in range(nq):
                value = values[0:nbp, q * ne : (q + 1) * ne]
                for d in range(3):
                    term = jac_ref[p, q, d : d + 1, :] * value
                    sums[d] = term if q == 0 else sums[d] + term
            for d in range(3):
                coup[d * nbp : (d + 1) * nbp, lane] = sums[d]

    def first_sends():
        for load in loads_in[:3]:
            load.wait()
        h_hi, h_lo = split(height_ref[...])
        for layer in range(n_gz):

            @pl.when(k == layer)
            def _():
                for t in range(tiles):
                    span = slice(t * slots, (t + 1) * slots)
                    w_out[t, 0:nf, :] = weight_ref[0, :, layer, span]

        for number, piece in enumerate(pieces):
            hot = ones_where(in_col(k, piece))
            picked = mm(h_hi, hot) + mm(h_lo, hot)
            heights = jnp.sum(jnp.where(in_row(k, piece), picked, 0.0), axis=0, keepdims=True)
            for part in range(group):
                t = number * group + part
                w_out[t, nf : nf + 1, :] = heights[:, part * slots : (part + 1) * slots]

        flow_out[0] = east_ref[0:1, :]
        flow_out[1] = east_ref[rows - 1 : rows, :]
        flow_out[2] = as_row(north_ref[:, 0:1])
        flow_out[3] = as_row(north_ref[:, cols - 1 : cols])

        pl.semaphore_wait(barrier, devices - 1)

        @pl.loop(0, tiles)
        def _(t):
            @pl.when(t != tile)
            def _():
                weights_to(t, tile).start()

        start_exchange(flow_out, flow_in, o_send, o_recv, 4)
        w_in[tile] = w_out[tile]

    weight_now = time_step
    for degree in range(1, 5):
        couple(cur)
        weight_now = weight_now * time_step / (degree + 1)
        moved = halves(lhs_d, coup[...])
        if degree < 4:
            cur[...] = moved
        integ[0:nbp, :] += weight_now * moved
        if degree == 1:
            first_sends()

    traces = halves(lhs_p, integ[...])
    for q in range(nq):
        for f in range(4):
            table[q * nfp : (q + 1) * nfp, f * ne : (f + 1) * ne] = traces[
                f * nfp : (f + 1) * nfp, q * ne : (q + 1) * ne
            ]
    t_hi, t_lo = split(table[...])

    sends = 6 * block
    pick = ones_where(iota((sends, 6), 0) // block == iota((sends, 6), 1))
    index = send_ref[...]
    high = mm(pick, (index // 16).astype(F32).astype(BF16))
    low = mm(pick, (index % 16).astype(F32).astype(BF16))
    which = iota((sends, block), 0) % block == iota((sends, block), 1)
    chosen = jnp.sum(jnp.where(which, high * 16.0 + low, 0.0), axis=1, keepdims=True)
    send_hot = ones_where(iota((sends, 4 * ne), 1) == chosen.astype(jnp.int32))
    outgoing = mm(send_hot, t_hi, NT) + mm(send_hot, t_lo, NT)
    for direction in range(6):
        faces_out[direction] = outgoing[direction * block : (direction + 1) * block, :]
    start_exchange(faces_out, faces_in, f_send, f_recv, 6)

    for piece in pieces:
        floors = floor_ref[:, piece]
        floor_hot[:, piece] = ones_where(iota((4 * ne, floors.shape[1]), 0) == floors)
    vertical = slice((nq - 1) * nfp, nq * nfp)
    uptrace = mm(t_hi[vertical], floor_hot[...]) + mm(t_lo[vertical], floor_hot[...])

    @pl.loop(0, tiles)
    def _(t):
        @pl.when(t != tile)
        def _():
            weights_to(t, t).wait()

    for t in range(tiles):
        v_out[t] = jnp.sum(
            w_in[t, 0:nf, :] * uptrace[0:nf, t * slots : (t + 1) * slots], axis=0, keepdims=True
        )

    def values_to(n, slot):
        return pltpu.make_async_remote_copy(
            src_ref=v_out.at[n // n_gz],
            dst_ref=v_in.at[slot],
            send_sem=v_send.at[n],
            recv_sem=v_recv.at[slot],
            device_id=place(n),
            device_id_type=MESH,
        )

    mine = k * tiles + tile

    @pl.loop(0, devices)
    def _(n):
        @pl.when(n != me)
        def _():
            values_to(n, mine).start()

    v_in[mine] = v_out[tile]

    @pl.loop(0, n_gz)
    def _(layer):
        for span in pieces:
            hot_c[layer, :, span] = ones_where(in_col(layer, span))

    couple(integ)
    volume = halves(lhs_v, coup[...])

    loads_in[3].wait()
    @pl.loop(0, nq)
    def _(p):
        lane = pl.ds(pl.multiple_of(p * ne, ne), ne)
        for f in range(4):
            total = None
            for q in range(nq):
                own = table[q * nfp : (q + 1) * nfp, f * ne : (f + 1) * ne]
                term = self_ref[q, p, f : f + 1, :] * own
                total = term if q == 0 else total + term
            numeric[f * nfp : (f + 1) * nfp, lane] = total

    loads = jnp.concatenate(
        [w_in[t] * w_in[t, nf : nf + 1, :] for t in range(tiles)], axis=1
    )
    l_hi, l_lo = split(loads)
    face_load = mm(l_hi, floor_hot[...], NT) + mm(l_lo, floor_hot[...], NT)
    for f in range(4):
        numeric[f * nfp : f * nfp + nf, 2 * ne : 3 * ne] += face_load[
            0:nf, f * ne : (f + 1) * ne
        ]

    end_exchange(flow_out, flow_in, o_send, o_recv, 4)
    slope_x, slope_y = slopers(rows, cols)
    loads_in[4].wait()
    slopes = slope_x(east_ref[...], flow_in) + slope_y(north_ref[...], flow_in)
    base = height_ref[...] - ocean_step * (depth_ref[...] * slopes)

    @pl.loop(0, devices)
    def _(n):
        @pl.when(n != me)
        def _():
            values_to(n, (n % n_gz) * tiles + n // n_gz).wait()

    source = jnp.zeros((rows, cols), F32)
    for layer in range(n_gz):
        for number, piece in enumerate(pieces):
            first = layer * tiles + number * group
            values = jnp.concatenate([v_in[first + part] for part in range(group)], axis=1)
            v_hi, v_lo = split(values)
            here, other = in_row(layer, piece), hot_c[layer, :, piece]
            for part in (v_hi, v_lo):
                spread = jnp.where(here, part.astype(F32), 0.0).astype(BF16)
                source += mm(spread, other, NT)
    new_height = base + ocean_step * source
    rim_out[0] = new_height[0:1, :]
    rim_out[1] = new_height[rows - 1 : rows, :]
    rim_out[2] = as_row(new_height[:, 0:1])
    rim_out[3] = as_row(new_height[:, cols - 1 : cols])
    start_exchange(rim_out, rim_in, r_send, r_recv, 4)
    new_height_ref[...] = new_height

    loads_in[5].wait()
    for f in range(4):
        face_hot[:, f * ne : (f + 1) * ne] = ones_where(
            iota((face_hot.shape[0], ne), 0) == source_ref[f : f + 1, :]
        )
    hot_own = face_hot[0 : 4 * ne, :]
    remote = mm(t_hi, hot_own) + mm(t_lo, hot_own)
    end_exchange(faces_out, faces_in, f_send, f_recv, 6)
    arrived = jnp.concatenate([faces_in[direction] for direction in range(6)], axis=0)
    a_hi, a_lo = split(arrived)
    width = nq * nfp
    eye_t = ones_where(iota((width, width), 0) == iota((width, width), 1))
    hot_far = face_hot[4 * ne : 4 * ne + sends, :]
    remote = remote + mm(mm(eye_t, a_hi, NT).astype(BF16), hot_far)
    remote = remote + mm(mm(eye_t, a_lo, NT).astype(BF16), hot_far)
    table[...] = remote

    @pl.loop(0, nq)
    def _(p):
        lane = pl.ds(pl.multiple_of(p * ne, ne), ne)
        for f in range(4):
            total = numeric[f * nfp : (f + 1) * nfp, lane]
            for q in range(nq):
                far = table[q * nfp : (q + 1) * nfp, f * ne : (f + 1) * ne]
                total = total + other_ref[q, p, f : f + 1, :] * far
            numeric[f * nfp : (f + 1) * nfp, lane] = total

    change_ref[...] = volume - halves(lhs_t, numeric[...])
    end_exchange(rim_out, rim_in, r_send, r_recv, 4)
    rim_ref[...] = rim_in[...]


def finish(
    state_ref,
    mask_ref,
    change_ref,
    height_ref,
    rim_ref,
    east_ref,
    north_ref,
    next_ref,
    new_height_ref,
    new_east_ref,
    new_north_ref,
):
    nq, nb, ne = state_ref.shape
    finest = mask_ref[...] > 0
    for q in range(nq):
        state = state_ref[q]
        change = change_ref[0:nb, q * ne : (q + 1) * ne]
        next_ref[q] = jnp.where(finest, state + change, state)
    slope_x, slope_y = slopers(*height_ref.shape)
    height = height_ref[...]
    new_height_ref[...] = height
    new_east_ref[...] = east_ref[...] - ocean_step * slope_x(height, rim_ref)
    new_north_ref[...] = north_ref[...] - ocean_step * slope_y(height, rim_ref)


def on_device(
    sizes,
    element_state,
    jacobians,
    stiffness,
    projection,
    flux_self,
    flux_other,
    face_source,
    send_faces,
    cluster_mask,
    seafloor_face,
    ocean_cell,
    ocean_weight,
    height,
    east_flow,
    north_flow,
    water_depth,
):
    n_gx, n_gy, n_gz = sizes
    nq, nb, ne = element_state.shape
    nf = projection.shape[1]
    tiles = n_gx * n_gy
    devices = tiles * n_gz
    slots = seafloor_face.shape[0] // tiles
    block = send_faces.shape[1]
    rows, cols = height.shape
    nbp, nfp = up(nb, 8), up(nf, 16)
    half = up(3 * nbp, 16)
    nbk = up(nb, 16)
    faces = 4 * nfp
    args = (
        element_state,
        jnp.transpose(jacobians, (1, 2, 0, 3)),
        stiffness,
        jnp.transpose(projection, (1, 0, 2)),
        jnp.transpose(flux_self, (1, 2, 0, 3)),
        jnp.transpose(flux_other, (1, 2, 0, 3)),
        face_source,
        send_faces,
        seafloor_face.reshape(1, -1),
        ocean_cell,
        jnp.transpose(ocean_weight, (0, 2, 1, 3)),
        height,
        east_flow,
        north_flow,
        water_depth,
    )
    scratch = [
        pltpu.VMEM((nbp, nq * ne), F32),
        pltpu.VMEM((nbk, nq * ne), F32),
        pltpu.VMEM((half, nq * ne), F32),
        pltpu.VMEM((2 * nbp, 2 * half), F32),
        pltpu.VMEM((2 * nbp, 2 * half), F32),
        pltpu.VMEM((2 * faces, 2 * nbk), F32),
        pltpu.VMEM((2 * nbp, 2 * faces), F32),
        pltpu.VMEM((nq * nfp, 4 * ne), F32),
        pltpu.VMEM((faces, nq * ne), F32),
        pltpu.VMEM((4 * ne, tiles * slots), BF16),
        pltpu.VMEM((up(4 * ne + 6 * block, 16), 4 * ne), BF16),
        pltpu.VMEM((n_gz, cols, tiles * slots), BF16),
        pltpu.VMEM((tiles, nfp, slots), F32),
        pltpu.VMEM((tiles, nfp, slots), F32),
        pltpu.VMEM((tiles, 1, slots), F32),
        pltpu.VMEM((devices, 1, slots), F32),
        pltpu.VMEM((6, block, nq * nfp), F32),
        pltpu.VMEM((6, block, nq * nfp), F32),
        pltpu.VMEM((4, 1, cols), F32),
        pltpu.VMEM((4, 1, cols), F32),
        pltpu.VMEM((4, 1, cols), F32),
        pltpu.VMEM((4, 1, cols), F32),
    ]
    for count in (tiles, devices, 6, 4, 4):
        scratch += [pltpu.SemaphoreType.DMA((count,)), pltpu.SemaphoreType.DMA((count,))]
    grid = pltpu.VMEM((rows, cols), F32)
    flux = pltpu.VMEM((nq, nq, 4, ne), F32)
    scratch += [flux, flux, grid, grid, grid, grid, pltpu.SemaphoreType.DMA((6,))]
    vmem, anywhere = pl.BlockSpec(memory_space=pltpu.VMEM), pl.BlockSpec(memory_space=pl.ANY)
    change, new_height, rim = pl.pallas_call(
        functools.partial(kernel, (n_gx, n_gy, n_gz, nq, nb, nf, ne, slots, block)),
        out_shape=(
            jax.ShapeDtypeStruct((nbp, nq * ne), F32),
            jax.ShapeDtypeStruct(height.shape, F32),
            jax.ShapeDtypeStruct((4, 1, cols), F32),
        ),
        in_specs=[vmem] * 4 + [anywhere] * 2 + [vmem] * 5 + [anywhere] * 4,
        out_specs=[vmem] * 3,
        scratch_shapes=scratch,
        compiler_params=pltpu.CompilerParams(collective_id=0, has_side_effects=True),
        name="step",
    )(*args)
    return pl.pallas_call(
        finish,
        out_shape=(
            jax.ShapeDtypeStruct(element_state.shape, F32),
            jax.ShapeDtypeStruct(height.shape, F32),
            jax.ShapeDtypeStruct(height.shape, F32),
            jax.ShapeDtypeStruct(height.shape, F32),
        ),
        in_specs=[vmem] * 7,
        out_specs=[vmem] * 4,
        name="finish",
    )(element_state, cluster_mask.reshape(1, -1), change, new_height, rim, east_flow, north_flow)


def solution(mesh):
    sizes = tuple(mesh.shape[axis] for axis in ("gx", "gy", "gz"))
    return jax.shard_map(
        functools.partial(on_device, sizes),
        mesh=mesh,
        in_specs=(
            P(None, None, ("gx", "gy", "gz")),
            P(None, None, None, ("gx", "gy", "gz")),
            P(),
            P(),
            P(None, None, None, ("gx", "gy", "gz")),
            P(None, None, None, ("gx", "gy", "gz")),
            P(None, ("gx", "gy", "gz")),
            P(None, ("gx", "gy", "gz")),
            P(("gx", "gy", "gz")),
            P(("gx", "gy", "gz")),
            P(("gx", "gy"), None, None),
            P(("gx", "gy"), None, None, None),
            P("gx", "gy"),
            P("gx", "gy"),
            P("gx", "gy"),
            P("gx", "gy"),
        ),
        out_specs=(P(None, None, ("gx", "gy", "gz")), P("gx", "gy"), P("gx", "gy"), P("gx", "gy")),
        check_vma=False,
    )
```

```python
import functools

import jax
import jax.numpy as jnp
from jax import lax
from jax.experimental import pallas as pl
from jax.experimental.pallas import tpu as pltpu
from jax.sharding import PartitionSpec as P

F32 = jnp.float32
BF16 = jnp.bfloat16
MESH = pl.DeviceIdType.MESH
time_step = 1.5
ocean_step = 0.5
NN = (((1,), (0,)), ((), ()))
NT = (((1,), (1,)), ((), ()))


def up(n, m):
    return -(-n // m) * m


def mm(a, b, dims=NN):
    return lax.dot_general(a, b, dims, preferred_element_type=F32)


def split(x):
    hi = x.astype(BF16)
    return hi, (x - hi.astype(F32)).astype(BF16)


def both(hi, lo, rhs, dims=NN):
    out = mm(jnp.concatenate([hi, lo], axis=0), rhs, dims)
    return out[: hi.shape[0]] + out[hi.shape[0] :]


def iota(shape, dim):
    return lax.broadcasted_iota(jnp.int32, shape, dim)


def ones_where(cond):
    return jnp.where(cond, 1.0, 0.0).astype(BF16)


def slopers(rows, cols):
    square = iota((rows, cols), 0) == iota((rows, cols), 1)

    def as_column(row):
        return jnp.sum(jnp.where(square, row, 0.0), axis=1, keepdims=True)

    first_row, last_row = iota((rows, cols), 0) == 0, iota((rows, cols), 0) == rows - 1
    first_col, last_col = iota((rows, cols), 1) == 0, iota((rows, cols), 1) == cols - 1

    def slope_x(grid, rim):
        before = jnp.where(first_row, rim[0], pltpu.roll(grid, 1, 0))
        after = jnp.where(last_row, rim[1], pltpu.roll(grid, rows - 1, 0))
        return (after - before) * 0.5

    def slope_y(grid, rim):
        before = jnp.where(first_col, as_column(rim[2]), pltpu.roll(grid, 1, 1))
        after = jnp.where(last_col, as_column(rim[3]), pltpu.roll(grid, cols - 1, 1))
        return (after - before) * 0.5

    return slope_x, slope_y


def kernel(
    dims,
    state_ref,
    jac_ref,
    stiff_ref,
    proj_ref,
    self_hbm,
    other_hbm,
    source_ref,
    send_ref,
    floor_ref,
    cell_ref,
    weight_ref,
    height_hbm,
    east_hbm,
    north_hbm,
    depth_hbm,
    change_ref,
    new_height_ref,
    rim_ref,
    cur,
    integ,
    coup,
    lhs_d,
    lhs_v,
    lhs_p,
    lhs_t,
    table,
    numeric,
    floor_hot,
    face_hot,
    hot_c,
    w_out,
    w_in,
    v_out,
    v_in,
    faces_out,
    faces_in,
    flow_out,
    flow_in,
    rim_out,
    rim_in,
    w_send,
    w_recv,
    v_send,
    v_recv,
    f_send,
    f_recv,
    o_send,
    o_recv,
    r_send,
    r_recv,
    self_ref,
    other_ref,
    height_ref,
    east_ref,
    north_ref,
    depth_ref,
    in_sem,
):
    n_gx, n_gy, n_gz, nq, nb, nf, ne, slots, block = dims
    tiles = n_gx * n_gy
    devices = tiles * n_gz
    nbp, nfp = up(nb, 8), up(nf, 16)
    rows, cols = height_ref.shape
    i, j, k = lax.axis_index("gx"), lax.axis_index("gy"), lax.axis_index("gz")
    tile = i * n_gy + j
    half = coup.shape[0]

    def everyone(act):
        @pl.loop(0, n_gx)
        def _(a):
            @pl.loop(0, n_gy)
            def _(b):
                there = a * n_gy + b
                for c in range(n_gz):

                    @pl.when((there != tile) | (k != c))
                    def _():
                        act(a, b, c, there)

    def other_tiles(act):
        @pl.loop(0, n_gx)
        def _(a):
            for b in range(n_gy):

                @pl.when(a * n_gy + b != tile)
                def _():
                    act(a, b)

    barrier = pltpu.get_barrier_semaphore()

    everyone(
        lambda a, b, c, t: pl.semaphore_signal(
            barrier, inc=1, device_id=(a, b, c), device_id_type=MESH
        )
    )

    loads_in = [
        pltpu.make_async_copy(source, target, in_sem.at[number])
        for number, (source, target) in enumerate(
            (
                (height_hbm, height_ref),
                (east_hbm, east_ref),
                (north_hbm, north_ref),
                (self_hbm, self_ref),
                (depth_hbm, depth_ref),
                (other_hbm, other_ref),
            )
        )
    ]
    for load in loads_in:
        load.start()

    tile_slots = tiles * slots
    group = min(tiles, 8)
    pieces = [slice(t * slots, (t + group) * slots) for t in range(0, tiles, group)]

    def in_row(layer, span):
        cells = cell_ref[0, pl.ds(layer, 1), span]
        return iota((rows, cells.shape[1]), 0) == cells // cols

    def in_col(layer, span):
        cells = cell_ref[0, pl.ds(layer, 1), span]
        return iota((cols, cells.shape[1]), 0) == cells % cols

    square = iota((rows, cols), 0) == iota((rows, cols), 1)

    def as_row(column):
        return jnp.sum(jnp.where(square, column, 0.0), axis=0, keepdims=True)

    there = (i > 0, i < n_gx - 1, j > 0, j < n_gy - 1, k > 0, k < n_gz - 1)
    who = ((i - 1, j, k), (i + 1, j, k), (i, j - 1, k), (i, j + 1, k), (i, j, k - 1), (i, j, k + 1))

    def exchange(out, into, send, recv, direction):
        return pltpu.make_async_remote_copy(
            src_ref=out.at[direction],
            dst_ref=into.at[direction ^ 1],
            send_sem=send.at[direction],
            recv_sem=recv.at[direction ^ 1],
            device_id=who[direction],
            device_id_type=MESH,
        )

    def start_exchange(out, into, send, recv, count):
        for direction in range(count):

            @pl.when(there[direction])
            def _():
                exchange(out, into, send, recv, direction).start()

            @pl.when(jnp.logical_not(there[direction]))
            def _():
                into[direction] = jnp.zeros(into.shape[1:], F32)

    def end_exchange(out, into, send, recv, count):
        for direction in range(count):

            @pl.when(there[direction])
            def _():
                exchange(out, into, send, recv, direction).wait_send()
                pltpu.make_async_remote_copy(
                    src_ref=out.at[direction],
                    dst_ref=into.at[direction],
                    send_sem=send.at[direction],
                    recv_sem=recv.at[direction],
                    device_id=who[direction],
                    device_id_type=MESH,
                ).wait_recv()

    def weights_to(a, b, slot):
        t = a * n_gy + b
        return pltpu.make_async_remote_copy(
            src_ref=w_out.at[t],
            dst_ref=w_in.at[slot],
            send_sem=w_send.at[t],
            recv_sem=w_recv.at[slot],
            device_id=(a, b, k),
            device_id_type=MESH,
        )

    for ref in (lhs_d, lhs_v, lhs_p, lhs_t, coup, cur, integ):
        ref[...] = jnp.zeros(ref.shape, ref.dtype)
    eye_b = ones_where(iota((nbp, nb), 0) == iota((nbp, nb), 1))

    def spots(count, width, first, second):
        r, c = iota((count, width), 0), iota((count, width), 1)
        once = c == first + r
        return ones_where(once | (c == second + r)), ones_where(once)

    total_d = jnp.zeros((nbp, 2 * half), F32)
    total_dl, total_v, total_vl = total_d, total_d, total_d
    for d in range(3):
        pair, once = spots(nb, 2 * half, d * nbp, half + d * nbp)
        s_hi, s_lo = split(stiff_ref[d])
        total_d += mm(mm(eye_b, s_hi).astype(BF16), pair)
        total_dl += mm(mm(eye_b, s_lo).astype(BF16), once)
        total_v += mm(mm(eye_b, s_hi, NT).astype(BF16), pair)
        total_vl += mm(mm(eye_b, s_lo, NT).astype(BF16), once)
    lhs_d[0:nbp, :] = -total_d
    lhs_d[nbp : 2 * nbp, :] = -total_dl
    lhs_v[0:nbp, :] = total_v
    lhs_v[nbp : 2 * nbp, :] = total_vl

    nbk = integ.shape[0]
    faces = 4 * nfp
    both_b, once_b = spots(nb, 2 * nbk, 0, nbk)
    total_t = jnp.zeros((nbp, 2 * faces), F32)
    total_tl = total_t
    for f in range(4):
        pair, once = spots(nf, 2 * faces, f * nfp, faces + f * nfp)
        p_hi, p_lo = split(proj_ref[:, f, :])
        lhs_p[f * nfp : f * nfp + nf, :] = mm(p_hi, both_b)
        lhs_p[faces + f * nfp : faces + f * nfp + nf, :] = mm(p_lo, once_b)
        total_t += mm(mm(eye_b, p_hi, NT).astype(BF16), pair)
        total_tl += mm(mm(eye_b, p_lo, NT).astype(BF16), once)
    lhs_t[0:nbp, :] = total_t
    lhs_t[nbp : 2 * nbp, :] = total_tl

    def halves(lhs, rhs):
        hi, lo = split(rhs)
        out = mm(lhs[...].astype(BF16), jnp.concatenate([hi, lo], axis=0))
        count = out.shape[0] // 2
        return out[:count] + out[count:]

    for q in range(nq):
        cur[0:nb, q * ne : (q + 1) * ne] = state_ref[q]
    integ[0:nbp, :] = time_step * cur[...]

    def couple(values):
        @pl.loop(0, nq)
        def _(p):
            lane = pl.ds(pl.multiple_of(p * ne, ne), ne)
            sums = [None] * 3
            for q in range(nq):
                value = values[0:nbp, q * ne : (q + 1) * ne]
                for d in range(3):
                    term = jac_ref[p, q, d : d + 1, :] * value
                    sums[d] = term if q == 0 else sums[d] + term
            for d in range(3):
                coup[d * nbp : (d + 1) * nbp, lane] = sums[d]

    def first_sends():
        for load in loads_in[:3]:
            load.wait()
        h_hi, h_lo = split(height_ref[...])
        for layer in range(n_gz):

            @pl.when(k == layer)
            def _():
                for t in range(tiles):
                    span = slice(t * slots, (t + 1) * slots)
                    w_out[t, 0:nf, :] = weight_ref[0, :, layer, span]

        for number, piece in enumerate(pieces):
            hot = ones_where(in_col(k, piece))
            picked = both(h_hi, h_lo, hot)
            heights = jnp.sum(jnp.where(in_row(k, piece), picked, 0.0), axis=0, keepdims=True)
            for part in range(group):
                t = number * group + part
                w_out[t, nf : nf + 1, :] = heights[:, part * slots : (part + 1) * slots]

        flow_out[0] = east_ref[0:1, :]
        flow_out[1] = east_ref[rows - 1 : rows, :]
        flow_out[2] = as_row(north_ref[:, 0:1])
        flow_out[3] = as_row(north_ref[:, cols - 1 : cols])

        pl.semaphore_wait(barrier, devices - 1)

        other_tiles(lambda a, b: weights_to(a, b, tile).start())

        start_exchange(flow_out, flow_in, o_send, o_recv, 4)
        w_in[tile] = w_out[tile]

    weight_now = time_step
    for degree in range(1, 5):
        couple(cur)
        weight_now = weight_now * time_step / (degree + 1)
        moved = halves(lhs_d, coup[...])
        if degree < 4:
            cur[...] = moved
        integ[0:nbp, :] += weight_now * moved
        if degree == 1:
            first_sends()

    traces = halves(lhs_p, integ[...])
    for q in range(nq):
        for f in range(4):
            table[q * nfp : (q + 1) * nfp, f * ne : (f + 1) * ne] = traces[
                f * nfp : (f + 1) * nfp, q * ne : (q + 1) * ne
            ]
    t_hi, t_lo = split(table[...])

    sends = 6 * block
    pick = ones_where(iota((sends, 6), 0) // block == iota((sends, 6), 1))
    index = send_ref[...]
    high = mm(pick, (index // 16).astype(F32).astype(BF16))
    low = mm(pick, (index % 16).astype(F32).astype(BF16))
    which = iota((sends, block), 0) % block == iota((sends, block), 1)
    chosen = jnp.sum(jnp.where(which, high * 16.0 + low, 0.0), axis=1, keepdims=True)
    send_hot = ones_where(iota((sends, 4 * ne), 1) == chosen.astype(jnp.int32))
    outgoing = mm(send_hot, t_hi, NT) + mm(send_hot, t_lo, NT)
    for direction in range(6):
        faces_out[direction] = outgoing[direction * block : (direction + 1) * block, :]
    start_exchange(faces_out, faces_in, f_send, f_recv, 6)

    for piece in pieces:
        floors = floor_ref[:, piece]
        floor_hot[:, piece] = ones_where(iota((4 * ne, floors.shape[1]), 0) == floors)
    vertical = slice((nq - 1) * nfp, nq * nfp)
    uptrace = both(t_hi[vertical], t_lo[vertical], floor_hot[...])

    other_tiles(lambda a, b: weights_to(a, b, a * n_gy + b).wait())

    for t in range(tiles):
        v_out[t] = jnp.sum(
            w_in[t, 0:nf, :] * uptrace[0:nf, t * slots : (t + 1) * slots], axis=0, keepdims=True
        )

    def values_to(a, b, c, t, slot):
        return pltpu.make_async_remote_copy(
            src_ref=v_out.at[t],
            dst_ref=v_in.at[slot],
            send_sem=v_send.at[c * tiles + t],
            recv_sem=v_recv.at[slot],
            device_id=(a, b, c),
            device_id_type=MESH,
        )

    mine = k * tiles + tile

    everyone(lambda a, b, c, t: values_to(a, b, c, t, mine).start())

    v_in[mine] = v_out[tile]

    @pl.loop(0, n_gz)
    def _(layer):
        for span in pieces:
            hot_c[layer, :, span] = ones_where(in_col(layer, span))

    couple(integ)
    volume = halves(lhs_v, coup[...])

    loads_in[3].wait()
    @pl.loop(0, nq)
    def _(p):
        lane = pl.ds(pl.multiple_of(p * ne, ne), ne)
        for f in range(4):
            total = None
            for q in range(nq):
                own = table[q * nfp : (q + 1) * nfp, f * ne : (f + 1) * ne]
                term = self_ref[q, p, f : f + 1, :] * own
                total = term if q == 0 else total + term
            numeric[f * nfp : (f + 1) * nfp, lane] = total

    loads = jnp.concatenate(
        [w_in[t] * w_in[t, nf : nf + 1, :] for t in range(tiles)], axis=1
    )
    l_hi, l_lo = split(loads)
    face_load = both(l_hi, l_lo, floor_hot[...], NT)
    for f in range(4):
        numeric[f * nfp : f * nfp + nf, 2 * ne : 3 * ne] += face_load[
            0:nf, f * ne : (f + 1) * ne
        ]

    end_exchange(flow_out, flow_in, o_send, o_recv, 4)
    slope_x, slope_y = slopers(rows, cols)
    loads_in[4].wait()
    slopes = slope_x(east_ref[...], flow_in) + slope_y(north_ref[...], flow_in)
    base = height_ref[...] - ocean_step * (depth_ref[...] * slopes)

    everyone(lambda a, b, c, t: values_to(a, b, c, t, c * tiles + t).wait())

    new_height_ref[...] = base

    @pl.loop(0, n_gz)
    def _(layer):
        for number, piece in enumerate(pieces):
            first = layer * tiles + number * group
            values = jnp.concatenate([v_in[first + part] for part in range(group)], axis=1)
            here = in_row(layer, piece)
            v_hi, v_lo = (
                jnp.where(here, part.astype(F32), 0.0).astype(BF16) for part in split(values)
            )
            new_height_ref[...] += ocean_step * both(v_hi, v_lo, hot_c[layer, :, piece], NT)

    new_height = new_height_ref[...]
    rim_out[0] = new_height[0:1, :]
    rim_out[1] = new_height[rows - 1 : rows, :]
    rim_out[2] = as_row(new_height[:, 0:1])
    rim_out[3] = as_row(new_height[:, cols - 1 : cols])
    start_exchange(rim_out, rim_in, r_send, r_recv, 4)
    loads_in[5].wait()
    for f in range(4):
        face_hot[:, f * ne : (f + 1) * ne] = ones_where(
            iota((face_hot.shape[0], ne), 0) == source_ref[f : f + 1, :]
        )
    hot_own = face_hot[0 : 4 * ne, :]
    remote = both(t_hi, t_lo, hot_own)
    end_exchange(faces_out, faces_in, f_send, f_recv, 6)
    arrived = jnp.concatenate([faces_in[direction] for direction in range(6)], axis=0)
    a_hi, a_lo = split(arrived)
    width = nq * nfp
    eye_t = ones_where(iota((width, width), 0) == iota((width, width), 1))
    hot_far = face_hot[4 * ne : 4 * ne + sends, :]
    remote = remote + mm(mm(eye_t, a_hi, NT).astype(BF16), hot_far)
    remote = remote + mm(mm(eye_t, a_lo, NT).astype(BF16), hot_far)
    table[...] = remote

    @pl.loop(0, nq)
    def _(p):
        lane = pl.ds(pl.multiple_of(p * ne, ne), ne)
        for f in range(4):
            total = numeric[f * nfp : (f + 1) * nfp, lane]
            for q in range(nq):
                far = table[q * nfp : (q + 1) * nfp, f * ne : (f + 1) * ne]
                total = total + other_ref[q, p, f : f + 1, :] * far
            numeric[f * nfp : (f + 1) * nfp, lane] = total

    change_ref[...] = volume - halves(lhs_t, numeric[...])
    end_exchange(rim_out, rim_in, r_send, r_recv, 4)
    rim_ref[...] = rim_in[...]


def finish(
    state_ref,
    mask_ref,
    change_ref,
    height_ref,
    rim_ref,
    east_ref,
    north_ref,
    next_ref,
    new_height_ref,
    new_east_ref,
    new_north_ref,
):
    nq, nb, ne = state_ref.shape
    finest = mask_ref[...] > 0
    for q in range(nq):
        state = state_ref[q]
        change = change_ref[0:nb, q * ne : (q + 1) * ne]
        next_ref[q] = jnp.where(finest, state + change, state)
    slope_x, slope_y = slopers(*height_ref.shape)
    height = height_ref[...]
    new_height_ref[...] = height
    new_east_ref[...] = east_ref[...] - ocean_step * slope_x(height, rim_ref)
    new_north_ref[...] = north_ref[...] - ocean_step * slope_y(height, rim_ref)


def on_device(
    sizes,
    element_state,
    jacobians,
    stiffness,
    projection,
    flux_self,
    flux_other,
    face_source,
    send_faces,
    cluster_mask,
    seafloor_face,
    ocean_cell,
    ocean_weight,
    height,
    east_flow,
    north_flow,
    water_depth,
):
    n_gx, n_gy, n_gz = sizes
    nq, nb, ne = element_state.shape
    nf = projection.shape[1]
    tiles = n_gx * n_gy
    devices = tiles * n_gz
    slots = seafloor_face.shape[0] // tiles
    block = send_faces.shape[1]
    rows, cols = height.shape
    nbp, nfp = up(nb, 8), up(nf, 16)
    half = up(3 * nbp, 16)
    nbk = up(nb, 16)
    faces = 4 * nfp
    args = (
        element_state,
        jnp.transpose(jacobians, (1, 2, 0, 3)),
        stiffness,
        jnp.transpose(projection, (1, 0, 2)),
        jnp.transpose(flux_self, (1, 2, 0, 3)),
        jnp.transpose(flux_other, (1, 2, 0, 3)),
        face_source,
        send_faces,
        seafloor_face.reshape(1, -1),
        ocean_cell,
        jnp.transpose(ocean_weight, (0, 2, 1, 3)),
        height,
        east_flow,
        north_flow,
        water_depth,
    )
    scratch = [
        pltpu.VMEM((nbp, nq * ne), F32),
        pltpu.VMEM((nbk, nq * ne), F32),
        pltpu.VMEM((half, nq * ne), F32),
        pltpu.VMEM((2 * nbp, 2 * half), F32),
        pltpu.VMEM((2 * nbp, 2 * half), F32),
        pltpu.VMEM((2 * faces, 2 * nbk), F32),
        pltpu.VMEM((2 * nbp, 2 * faces), F32),
        pltpu.VMEM((nq * nfp, 4 * ne), F32),
        pltpu.VMEM((faces, nq * ne), F32),
        pltpu.VMEM((4 * ne, tiles * slots), BF16),
        pltpu.VMEM((up(4 * ne + 6 * block, 16), 4 * ne), BF16),
        pltpu.VMEM((n_gz, cols, tiles * slots), BF16),
        pltpu.VMEM((tiles, nfp, slots), F32),
        pltpu.VMEM((tiles, nfp, slots), F32),
        pltpu.VMEM((tiles, 1, slots), F32),
        pltpu.VMEM((devices, 1, slots), F32),
        pltpu.VMEM((6, block, nq * nfp), F32),
        pltpu.VMEM((6, block, nq * nfp), F32),
        pltpu.VMEM((4, 1, cols), F32),
        pltpu.VMEM((4, 1, cols), F32),
        pltpu.VMEM((4, 1, cols), F32),
        pltpu.VMEM((4, 1, cols), F32),
    ]
    for count in (tiles, devices, 6, 4, 4):
        scratch += [pltpu.SemaphoreType.DMA((count,)), pltpu.SemaphoreType.DMA((count,))]
    grid = pltpu.VMEM((rows, cols), F32)
    flux = pltpu.VMEM((nq, nq, 4, ne), F32)
    scratch += [flux, flux, grid, grid, grid, grid, pltpu.SemaphoreType.DMA((6,))]
    vmem, anywhere = pl.BlockSpec(memory_space=pltpu.VMEM), pl.BlockSpec(memory_space=pl.ANY)
    change, new_height, rim = pl.pallas_call(
        functools.partial(kernel, (n_gx, n_gy, n_gz, nq, nb, nf, ne, slots, block)),
        out_shape=(
            jax.ShapeDtypeStruct((nbp, nq * ne), F32),
            jax.ShapeDtypeStruct(height.shape, F32),
            jax.ShapeDtypeStruct((4, 1, cols), F32),
        ),
        in_specs=[vmem] * 4 + [anywhere] * 2 + [vmem] * 5 + [anywhere] * 4,
        out_specs=[vmem] * 3,
        scratch_shapes=scratch,
        compiler_params=pltpu.CompilerParams(collective_id=0, has_side_effects=True),
        name="step",
    )(*args)
    return pl.pallas_call(
        finish,
        out_shape=(
            jax.ShapeDtypeStruct(element_state.shape, F32),
            jax.ShapeDtypeStruct(height.shape, F32),
            jax.ShapeDtypeStruct(height.shape, F32),
            jax.ShapeDtypeStruct(height.shape, F32),
        ),
        in_specs=[vmem] * 7,
        out_specs=[vmem] * 4,
        name="finish",
    )(element_state, cluster_mask.reshape(1, -1), change, new_height, rim, east_flow, north_flow)


def solution(mesh):
    sizes = tuple(mesh.shape[axis] for axis in ("gx", "gy", "gz"))
    return jax.shard_map(
        functools.partial(on_device, sizes),
        mesh=mesh,
        in_specs=(
            P(None, None, ("gx", "gy", "gz")),
            P(None, None, None, ("gx", "gy", "gz")),
            P(),
            P(),
            P(None, None, None, ("gx", "gy", "gz")),
            P(None, None, None, ("gx", "gy", "gz")),
            P(None, ("gx", "gy", "gz")),
            P(None, ("gx", "gy", "gz")),
            P(("gx", "gy", "gz")),
            P(("gx", "gy", "gz")),
            P(("gx", "gy"), None, None),
            P(("gx", "gy"), None, None, None),
            P("gx", "gy"),
            P("gx", "gy"),
            P("gx", "gy"),
            P("gx", "gy"),
        ),
        out_specs=(P(None, None, ("gx", "gy", "gz")), P("gx", "gy"), P("gx", "gy"), P("gx", "gy")),
        check_vma=False,
    )
```

```python
import functools

import jax
import jax.numpy as jnp
from jax import lax
from jax.experimental import pallas as pl
from jax.experimental.pallas import tpu as pltpu
from jax.sharding import PartitionSpec as P

F32 = jnp.float32
BF16 = jnp.bfloat16
MESH = pl.DeviceIdType.MESH
time_step = 1.5
ocean_step = 0.5
NN = (((1,), (0,)), ((), ()))
NT = (((1,), (1,)), ((), ()))


def up(n, m):
    return -(-n // m) * m


def mm(a, b, dims=NN):
    return lax.dot_general(a, b, dims, preferred_element_type=F32)


def split(x):
    hi = x.astype(BF16)
    return hi, (x - hi.astype(F32)).astype(BF16)


def both(hi, lo, rhs, dims=NN):
    out = mm(jnp.concatenate([hi, lo], axis=0), rhs, dims)
    return out[: hi.shape[0]] + out[hi.shape[0] :]


def iota(shape, dim):
    return lax.broadcasted_iota(jnp.int32, shape, dim)


def ones_where(cond):
    return jnp.where(cond, 1.0, 0.0).astype(BF16)


def slopers(rows, cols):
    square = iota((rows, cols), 0) == iota((rows, cols), 1)

    def as_column(row):
        return jnp.sum(jnp.where(square, row, 0.0), axis=1, keepdims=True)

    first_row, last_row = iota((rows, cols), 0) == 0, iota((rows, cols), 0) == rows - 1
    first_col, last_col = iota((rows, cols), 1) == 0, iota((rows, cols), 1) == cols - 1

    def slope_x(grid, rim):
        before = jnp.where(first_row, rim[0], pltpu.roll(grid, 1, 0))
        after = jnp.where(last_row, rim[1], pltpu.roll(grid, rows - 1, 0))
        return (after - before) * 0.5

    def slope_y(grid, rim):
        before = jnp.where(first_col, as_column(rim[2]), pltpu.roll(grid, 1, 1))
        after = jnp.where(last_col, as_column(rim[3]), pltpu.roll(grid, cols - 1, 1))
        return (after - before) * 0.5

    return slope_x, slope_y


def kernel(
    dims,
    state_ref,
    jac_ref,
    stiff_ref,
    proj_ref,
    self_hbm,
    other_hbm,
    source_ref,
    send_ref,
    floor_ref,
    cell_ref,
    weight_ref,
    height_hbm,
    east_hbm,
    north_hbm,
    depth_hbm,
    change_ref,
    new_height_ref,
    rim_ref,
    cur,
    integ,
    coup,
    lhs_d,
    lhs_v,
    lhs_p,
    lhs_t,
    table,
    numeric,
    floor_hot,
    face_hot,
    hot_c,
    w_out,
    w_in,
    v_out,
    v_in,
    faces_out,
    faces_in,
    flow_out,
    flow_in,
    rim_out,
    rim_in,
    w_send,
    w_recv,
    v_send,
    v_recv,
    f_send,
    f_recv,
    o_send,
    o_recv,
    r_send,
    r_recv,
    self_ref,
    other_ref,
    height_ref,
    east_ref,
    north_ref,
    depth_ref,
    in_sem,
):
    n_gx, n_gy, n_gz, nq, nb, nf, ne, slots, block = dims
    tiles = n_gx * n_gy
    devices = tiles * n_gz
    nbp, nfp = up(nb, 8), up(nf, 16)
    rows, cols = height_ref.shape
    i, j, k = lax.axis_index("gx"), lax.axis_index("gy"), lax.axis_index("gz")
    tile = i * n_gy + j
    half = coup.shape[0]

    def everyone(act):
        @pl.loop(0, n_gx)
        def _(a):
            @pl.loop(0, n_gy)
            def _(b):
                there = a * n_gy + b
                for c in range(n_gz):

                    @pl.when((there != tile) | (k != c))
                    def _():
                        act(a, b, c, there)

    def other_tiles(act):
        @pl.loop(0, n_gx)
        def _(a):
            for b in range(n_gy):

                @pl.when(a * n_gy + b != tile)
                def _():
                    act(a, b)

    barrier = pltpu.get_barrier_semaphore()

    everyone(
        lambda a, b, c, t: pl.semaphore_signal(
            barrier, inc=1, device_id=(a, b, c), device_id_type=MESH
        )
    )

    loads_in = [
        pltpu.make_async_copy(source, target, in_sem.at[number])
        for number, (source, target) in enumerate(
            (
                (height_hbm, height_ref),
                (east_hbm, east_ref),
                (north_hbm, north_ref),
                (self_hbm, self_ref),
                (depth_hbm, depth_ref),
                (other_hbm, other_ref),
            )
        )
    ]
    for load in loads_in:
        load.start()

    tile_slots = tiles * slots
    group = min(tiles, 8)
    pieces = [slice(t * slots, (t + group) * slots) for t in range(0, tiles, group)]

    def in_row(layer, span):
        cells = cell_ref[0, pl.ds(layer, 1), span]
        return iota((rows, cells.shape[1]), 0) == cells // cols

    def in_col(layer, span):
        cells = cell_ref[0, pl.ds(layer, 1), span]
        return iota((cols, cells.shape[1]), 0) == cells % cols

    square = iota((rows, cols), 0) == iota((rows, cols), 1)

    def as_row(column):
        return jnp.sum(jnp.where(square, column, 0.0), axis=0, keepdims=True)

    there = (i > 0, i < n_gx - 1, j > 0, j < n_gy - 1, k > 0, k < n_gz - 1)
    who = ((i - 1, j, k), (i + 1, j, k), (i, j - 1, k), (i, j + 1, k), (i, j, k - 1), (i, j, k + 1))

    def exchange(out, into, send, recv, direction):
        return pltpu.make_async_remote_copy(
            src_ref=out.at[direction],
            dst_ref=into.at[direction ^ 1],
            send_sem=send.at[direction],
            recv_sem=recv.at[direction ^ 1],
            device_id=who[direction],
            device_id_type=MESH,
        )

    def start_exchange(out, into, send, recv, count):
        for direction in range(count):

            @pl.when(there[direction])
            def _():
                exchange(out, into, send, recv, direction).start()

            @pl.when(jnp.logical_not(there[direction]))
            def _():
                into[direction] = jnp.zeros(into.shape[1:], F32)

    def end_exchange(out, into, send, recv, count):
        for direction in range(count):

            @pl.when(there[direction])
            def _():
                exchange(out, into, send, recv, direction).wait_send()
                pltpu.make_async_remote_copy(
                    src_ref=out.at[direction],
                    dst_ref=into.at[direction],
                    send_sem=send.at[direction],
                    recv_sem=recv.at[direction],
                    device_id=who[direction],
                    device_id_type=MESH,
                ).wait_recv()

    def weights_to(a, b, slot):
        t = a * n_gy + b
        return pltpu.make_async_remote_copy(
            src_ref=w_out.at[t],
            dst_ref=w_in.at[slot],
            send_sem=w_send.at[t],
            recv_sem=w_recv.at[slot],
            device_id=(a, b, k),
            device_id_type=MESH,
        )

    for ref in (lhs_d, lhs_v, lhs_p, lhs_t, coup, cur, integ):
        ref[...] = jnp.zeros(ref.shape, ref.dtype)
    eye_b = ones_where(iota((nbp, nb), 0) == iota((nbp, nb), 1))

    def spots(count, width, first, second):
        r, c = iota((count, width), 0), iota((count, width), 1)
        once = c == first + r
        return ones_where(once | (c == second + r)), ones_where(once)

    total_d = jnp.zeros((nbp, 2 * half), F32)
    total_dl, total_v, total_vl = total_d, total_d, total_d
    for d in range(3):
        pair, once = spots(nb, 2 * half, d * nbp, half + d * nbp)
        s_hi, s_lo = split(stiff_ref[d])
        total_d += mm(mm(eye_b, s_hi).astype(BF16), pair)
        total_dl += mm(mm(eye_b, s_lo).astype(BF16), once)
        total_v += mm(mm(eye_b, s_hi, NT).astype(BF16), pair)
        total_vl += mm(mm(eye_b, s_lo, NT).astype(BF16), once)
    lhs_d[0:nbp, :] = -total_d
    lhs_d[nbp : 2 * nbp, :] = -total_dl
    lhs_v[0:nbp, :] = total_v
    lhs_v[nbp : 2 * nbp, :] = total_vl

    nbk = integ.shape[0]
    faces = 4 * nfp
    both_b, once_b = spots(nb, 2 * nbk, 0, nbk)
    total_t = jnp.zeros((nbp, 2 * faces), F32)
    total_tl = total_t
    for f in range(4):
        pair, once = spots(nf, 2 * faces, f * nfp, faces + f * nfp)
        p_hi, p_lo = split(proj_ref[:, f, :])
        lhs_p[f * nfp : f * nfp + nf, :] = mm(p_hi, both_b)
        lhs_p[faces + f * nfp : faces + f * nfp + nf, :] = mm(p_lo, once_b)
        total_t += mm(mm(eye_b, p_hi, NT).astype(BF16), pair)
        total_tl += mm(mm(eye_b, p_lo, NT).astype(BF16), once)
    lhs_t[0:nbp, :] = total_t
    lhs_t[nbp : 2 * nbp, :] = total_tl

    def halves(lhs, rhs):
        hi, lo = split(rhs)
        out = mm(lhs[...].astype(BF16), jnp.concatenate([hi, lo], axis=0))
        count = out.shape[0] // 2
        return out[:count] + out[count:]

    for q in range(nq):
        cur[0:nb, q * ne : (q + 1) * ne] = state_ref[q]
    integ[0:nbp, :] = time_step * cur[...]

    def couple(values):
        @pl.loop(0, nq)
        def _(p):
            lane = pl.ds(pl.multiple_of(p * ne, ne), ne)
            sums = [None] * 3
            for q in range(nq):
                value = values[0:nbp, q * ne : (q + 1) * ne]
                for d in range(3):
                    term = jac_ref[p, q, d : d + 1, :] * value
                    sums[d] = term if q == 0 else sums[d] + term
            for d in range(3):
                coup[d * nbp : (d + 1) * nbp, lane] = sums[d]

    def first_sends():
        for load in loads_in[:3]:
            load.wait()
        h_hi, h_lo = split(height_ref[...])
        for layer in range(n_gz):

            @pl.when(k == layer)
            def _():
                for t in range(tiles):
                    span = slice(t * slots, (t + 1) * slots)
                    w_out[t, 0:nf, :] = weight_ref[0, :, layer, span]

        for number, piece in enumerate(pieces):
            hot = ones_where(in_col(k, piece))
            picked = both(h_hi, h_lo, hot)
            heights = jnp.sum(jnp.where(in_row(k, piece), picked, 0.0), axis=0, keepdims=True)
            for part in range(group):
                t = number * group + part
                w_out[t, nf : nf + 1, :] = heights[:, part * slots : (part + 1) * slots]

        flow_out[0] = east_ref[0:1, :]
        flow_out[1] = east_ref[rows - 1 : rows, :]
        flow_out[2] = as_row(north_ref[:, 0:1])
        flow_out[3] = as_row(north_ref[:, cols - 1 : cols])

        pl.semaphore_wait(barrier, devices - 1)

        other_tiles(lambda a, b: weights_to(a, b, tile).start())

        start_exchange(flow_out, flow_in, o_send, o_recv, 4)
        w_in[tile] = w_out[tile]

    weight_now = time_step
    for degree in range(1, 5):
        couple(cur)
        weight_now = weight_now * time_step / (degree + 1)
        moved = halves(lhs_d, coup[...])
        if degree < 4:
            cur[...] = moved
        integ[0:nbp, :] += weight_now * moved
        if degree == 1:
            first_sends()

    traces = halves(lhs_p, integ[...])
    for q in range(nq):
        for f in range(4):
            table[q * nfp : (q + 1) * nfp, f * ne : (f + 1) * ne] = traces[
                f * nfp : (f + 1) * nfp, q * ne : (q + 1) * ne
            ]
    t_hi, t_lo = split(table[...])

    sends = 6 * block
    pick = ones_where(iota((sends, 6), 0) // block == iota((sends, 6), 1))
    index = send_ref[...]
    high = mm(pick, (index // 16).astype(F32).astype(BF16))
    low = mm(pick, (index % 16).astype(F32).astype(BF16))
    which = iota((sends, block), 0) % block == iota((sends, block), 1)
    chosen = jnp.sum(jnp.where(which, high * 16.0 + low, 0.0), axis=1, keepdims=True)
    send_hot = ones_where(iota((sends, 4 * ne), 1) == chosen.astype(jnp.int32))
    outgoing = mm(send_hot, t_hi, NT) + mm(send_hot, t_lo, NT)
    for direction in range(6):
        faces_out[direction] = outgoing[direction * block : (direction + 1) * block, :]
    start_exchange(faces_out, faces_in, f_send, f_recv, 6)

    for piece in pieces:
        floors = floor_ref[:, piece]
        floor_hot[:, piece] = ones_where(iota((4 * ne, floors.shape[1]), 0) == floors)
    vertical = slice((nq - 1) * nfp, nq * nfp)
    uptrace = both(t_hi[vertical], t_lo[vertical], floor_hot[...])

    other_tiles(lambda a, b: weights_to(a, b, a * n_gy + b).wait())

    for t in range(tiles):
        v_out[t] = jnp.sum(
            w_in[t, 0:nf, :] * uptrace[0:nf, t * slots : (t + 1) * slots], axis=0, keepdims=True
        )

    def values_to(a, b, c, t, slot):
        return pltpu.make_async_remote_copy(
            src_ref=v_out.at[t],
            dst_ref=v_in.at[slot],
            send_sem=v_send.at[c * tiles + t],
            recv_sem=v_recv.at[slot],
            device_id=(a, b, c),
            device_id_type=MESH,
        )

    mine = k * tiles + tile

    everyone(lambda a, b, c, t: values_to(a, b, c, t, mine).start())

    v_in[mine] = v_out[tile]

    @pl.loop(0, n_gz)
    def _(layer):
        for span in pieces:
            hot_c[layer, :, span] = ones_where(in_col(layer, span))

    couple(integ)
    volume = halves(lhs_v, coup[...])

    loads_in[3].wait()
    @pl.loop(0, nq)
    def _(p):
        lane = pl.ds(pl.multiple_of(p * ne, ne), ne)
        for f in range(4):
            total = None
            for q in range(nq):
                own = table[q * nfp : (q + 1) * nfp, f * ne : (f + 1) * ne]
                term = self_ref[q, p, f : f + 1, :] * own
                total = term if q == 0 else total + term
            numeric[f * nfp : (f + 1) * nfp, lane] = total

    loads = jnp.concatenate(
        [w_in[t] * w_in[t, nf : nf + 1, :] for t in range(tiles)], axis=1
    )
    l_hi, l_lo = split(loads)
    face_load = both(l_hi, l_lo, floor_hot[...], NT)
    for f in range(4):
        numeric[f * nfp : f * nfp + nf, 2 * ne : 3 * ne] += face_load[
            0:nf, f * ne : (f + 1) * ne
        ]

    for f in range(4):
        face_hot[:, f * ne : (f + 1) * ne] = ones_where(
            iota((face_hot.shape[0], ne), 0) == source_ref[f : f + 1, :]
        )
    hot_own = face_hot[0 : 4 * ne, :]
    table[...] = both(t_hi, t_lo, hot_own)

    end_exchange(flow_out, flow_in, o_send, o_recv, 4)
    slope_x, slope_y = slopers(rows, cols)
    loads_in[4].wait()
    slopes = slope_x(east_ref[...], flow_in) + slope_y(north_ref[...], flow_in)
    base = height_ref[...] - ocean_step * (depth_ref[...] * slopes)

    everyone(lambda a, b, c, t: values_to(a, b, c, t, c * tiles + t).wait())

    new_height_ref[...] = base

    @pl.loop(0, n_gz)
    def _(layer):
        for number, piece in enumerate(pieces):
            first = layer * tiles + number * group
            values = jnp.concatenate([v_in[first + part] for part in range(group)], axis=1)
            here = in_row(layer, piece)
            v_hi, v_lo = (
                jnp.where(here, part.astype(F32), 0.0).astype(BF16) for part in split(values)
            )
            new_height_ref[...] += ocean_step * both(v_hi, v_lo, hot_c[layer, :, piece], NT)

    new_height = new_height_ref[...]
    rim_out[0] = new_height[0:1, :]
    rim_out[1] = new_height[rows - 1 : rows, :]
    rim_out[2] = as_row(new_height[:, 0:1])
    rim_out[3] = as_row(new_height[:, cols - 1 : cols])
    start_exchange(rim_out, rim_in, r_send, r_recv, 4)
    loads_in[5].wait()
    end_exchange(faces_out, faces_in, f_send, f_recv, 6)
    arrived = jnp.concatenate([faces_in[direction] for direction in range(6)], axis=0)
    a_hi, a_lo = split(arrived)
    width = nq * nfp
    eye_t = ones_where(iota((width, width), 0) == iota((width, width), 1))
    hot_far = face_hot[4 * ne : 4 * ne + sends, :]
    remote = table[...] + mm(mm(eye_t, a_hi, NT).astype(BF16), hot_far)
    remote = remote + mm(mm(eye_t, a_lo, NT).astype(BF16), hot_far)
    table[...] = remote

    @pl.loop(0, nq)
    def _(p):
        lane = pl.ds(pl.multiple_of(p * ne, ne), ne)
        for f in range(4):
            total = numeric[f * nfp : (f + 1) * nfp, lane]
            for q in range(nq):
                far = table[q * nfp : (q + 1) * nfp, f * ne : (f + 1) * ne]
                total = total + other_ref[q, p, f : f + 1, :] * far
            numeric[f * nfp : (f + 1) * nfp, lane] = total

    change_ref[...] = volume - halves(lhs_t, numeric[...])
    end_exchange(rim_out, rim_in, r_send, r_recv, 4)
    rim_ref[...] = rim_in[...]


def finish(
    state_ref,
    mask_ref,
    change_ref,
    height_ref,
    rim_ref,
    east_ref,
    north_ref,
    next_ref,
    new_height_ref,
    new_east_ref,
    new_north_ref,
):
    nq, nb, ne = state_ref.shape
    finest = mask_ref[...] > 0
    for q in range(nq):
        state = state_ref[q]
        change = change_ref[0:nb, q * ne : (q + 1) * ne]
        next_ref[q] = jnp.where(finest, state + change, state)
    slope_x, slope_y = slopers(*height_ref.shape)
    height = height_ref[...]
    new_height_ref[...] = height
    new_east_ref[...] = east_ref[...] - ocean_step * slope_x(height, rim_ref)
    new_north_ref[...] = north_ref[...] - ocean_step * slope_y(height, rim_ref)


def on_device(
    sizes,
    element_state,
    jacobians,
    stiffness,
    projection,
    flux_self,
    flux_other,
    face_source,
    send_faces,
    cluster_mask,
    seafloor_face,
    ocean_cell,
    ocean_weight,
    height,
    east_flow,
    north_flow,
    water_depth,
):
    n_gx, n_gy, n_gz = sizes
    nq, nb, ne = element_state.shape
    nf = projection.shape[1]
    tiles = n_gx * n_gy
    devices = tiles * n_gz
    slots = seafloor_face.shape[0] // tiles
    block = send_faces.shape[1]
    rows, cols = height.shape
    nbp, nfp = up(nb, 8), up(nf, 16)
    half = up(3 * nbp, 16)
    nbk = up(nb, 16)
    faces = 4 * nfp
    args = (
        element_state,
        jnp.transpose(jacobians, (1, 2, 0, 3)),
        stiffness,
        jnp.transpose(projection, (1, 0, 2)),
        jnp.transpose(flux_self, (1, 2, 0, 3)),
        jnp.transpose(flux_other, (1, 2, 0, 3)),
        face_source,
        send_faces,
        seafloor_face.reshape(1, -1),
        ocean_cell,
        jnp.transpose(ocean_weight, (0, 2, 1, 3)),
        height,
        east_flow,
        north_flow,
        water_depth,
    )
    scratch = [
        pltpu.VMEM((nbp, nq * ne), F32),
        pltpu.VMEM((nbk, nq * ne), F32),
        pltpu.VMEM((half, nq * ne), F32),
        pltpu.VMEM((2 * nbp, 2 * half), F32),
        pltpu.VMEM((2 * nbp, 2 * half), F32),
        pltpu.VMEM((2 * faces, 2 * nbk), F32),
        pltpu.VMEM((2 * nbp, 2 * faces), F32),
        pltpu.VMEM((nq * nfp, 4 * ne), F32),
        pltpu.VMEM((faces, nq * ne), F32),
        pltpu.VMEM((4 * ne, tiles * slots), BF16),
        pltpu.VMEM((up(4 * ne + 6 * block, 16), 4 * ne), BF16),
        pltpu.VMEM((n_gz, cols, tiles * slots), BF16),
        pltpu.VMEM((tiles, nfp, slots), F32),
        pltpu.VMEM((tiles, nfp, slots), F32),
        pltpu.VMEM((tiles, 1, slots), F32),
        pltpu.VMEM((devices, 1, slots), F32),
        pltpu.VMEM((6, block, nq * nfp), F32),
        pltpu.VMEM((6, block, nq * nfp), F32),
        pltpu.VMEM((4, 1, cols), F32),
        pltpu.VMEM((4, 1, cols), F32),
        pltpu.VMEM((4, 1, cols), F32),
        pltpu.VMEM((4, 1, cols), F32),
    ]
    for count in (tiles, devices, 6, 4, 4):
        scratch += [pltpu.SemaphoreType.DMA((count,)), pltpu.SemaphoreType.DMA((count,))]
    grid = pltpu.VMEM((rows, cols), F32)
    flux = pltpu.VMEM((nq, nq, 4, ne), F32)
    scratch += [flux, flux, grid, grid, grid, grid, pltpu.SemaphoreType.DMA((6,))]
    vmem, anywhere = pl.BlockSpec(memory_space=pltpu.VMEM), pl.BlockSpec(memory_space=pl.ANY)
    change, new_height, rim = pl.pallas_call(
        functools.partial(kernel, (n_gx, n_gy, n_gz, nq, nb, nf, ne, slots, block)),
        out_shape=(
            jax.ShapeDtypeStruct((nbp, nq * ne), F32),
            jax.ShapeDtypeStruct(height.shape, F32),
            jax.ShapeDtypeStruct((4, 1, cols), F32),
        ),
        in_specs=[vmem] * 4 + [anywhere] * 2 + [vmem] * 5 + [anywhere] * 4,
        out_specs=[vmem] * 3,
        scratch_shapes=scratch,
        compiler_params=pltpu.CompilerParams(collective_id=0, has_side_effects=True),
        name="step",
    )(*args)
    return pl.pallas_call(
        finish,
        out_shape=(
            jax.ShapeDtypeStruct(element_state.shape, F32),
            jax.ShapeDtypeStruct(height.shape, F32),
            jax.ShapeDtypeStruct(height.shape, F32),
            jax.ShapeDtypeStruct(height.shape, F32),
        ),
        in_specs=[vmem] * 7,
        out_specs=[vmem] * 4,
        name="finish",
    )(element_state, cluster_mask.reshape(1, -1), change, new_height, rim, east_flow, north_flow)


def solution(mesh):
    sizes = tuple(mesh.shape[axis] for axis in ("gx", "gy", "gz"))
    return jax.shard_map(
        functools.partial(on_device, sizes),
        mesh=mesh,
        in_specs=(
            P(None, None, ("gx", "gy", "gz")),
            P(None, None, None, ("gx", "gy", "gz")),
            P(),
            P(),
            P(None, None, None, ("gx", "gy", "gz")),
            P(None, None, None, ("gx", "gy", "gz")),
            P(None, ("gx", "gy", "gz")),
            P(None, ("gx", "gy", "gz")),
            P(("gx", "gy", "gz")),
            P(("gx", "gy", "gz")),
            P(("gx", "gy"), None, None),
            P(("gx", "gy"), None, None, None),
            P("gx", "gy"),
            P("gx", "gy"),
            P("gx", "gy"),
            P("gx", "gy"),
        ),
        out_specs=(P(None, None, ("gx", "gy", "gz")), P("gx", "gy"), P("gx", "gy"), P("gx", "gy")),
        check_vma=False,
    )
```
